128 devices in a mesh: ra: 32 (over y_lo, x, z), dec: 4 (over y_hi, core).
Axes of the slice: x: 4, y: 4 (y_hi: 2, y_lo: 2; y = y_hi * 2 + y_lo), z: 4, core: 2. Of those that a mesh axis runs over, the one named last changes fastest.
Arguments:
- lens_block: bfloat16 [32, 4, 130, 512], P('ra', 'dec'), may hold values from 0 to 255, as said below
- lens_count: int32 [32, 4], P('ra', 'dec'), may hold values from 64 to 512, as said below
- lens_region: int32 [32, 4, 512], P('ra', 'dec'), may hold values from 0 to 1023, as said below
- lens_sample: int32 [32, 4, 512], P('ra', 'dec'), may hold values from 0 to 7
- source_block: bfloat16 [32, 4, 133, 1024], P('ra', 'dec'), may hold values from -1 to 255, as said below
Outputs:
- jk_signal: float32 [1024, 8, 20], P(('ra', 'dec'))
- jk_weight: float32 [1024, 8, 20], P(('ra', 'dec'))
The draws below stay inside these ranges and needn't reach their ends.
Inputs may be any that keep to these rules, and one draw needn't show every extreme that they name: The live lenses of patch (i, j) fill its first lens_count[i, j] slots; each count is 512, 256, 128 or 64, and at least one patch is full. `lens_block`: the first 128 rows are zero or positive, and zero below the lens's own redshift bin; the last two rows are whole numbers from 0 to 255. `source_block`: the first 128 rows are zero or positive; positions are whole numbers from 0 to 255; weights are positive. `lens_region`: each id labels a compact area of the sky.
All inputs are finite; a program needn't handle non-finite values.
Results may differ from the reference program's by a relative error of at most 0.0003.
Values may be sent and summed in bfloat16 or wider, within the bound.
No kernel may reach another device: no remote copies, remote signals or barrier semaphores. Data moves between devices by JAX's collectives and lax.ppermute only.
A program may use at most 64 MiB of HBM per device.

```python
import math
import jax
import jax.numpy as jnp
from jax import lax

ZBINS = 128
NBIN = 20
SAMPLES = 8
PATCH = 256
R_IN = 12
L_PATCH = 512
S_PATCH = 1024
REG_DEV = 8
COLUMNS = 32
BANDS = 4
REGIONS = 1024


def lens_positions(key):
    key_x = jax.random.fold_in(key, 101)
    key_y = jax.random.fold_in(key, 102)
    position_x = jax.random.randint(key_x, (COLUMNS, BANDS, 1, L_PATCH), 0, PATCH)
    position_y = jax.random.randint(key_y, (COLUMNS, BANDS, 1, L_PATCH), 0, PATCH)
    return (position_x.astype(jnp.int32), position_y.astype(jnp.int32))


def draw_lens_count(key, part):
    key_levels, key_full = jax.random.split(key)
    halvings = jax.random.randint(key_levels, (COLUMNS, BANDS), 0, 4)
    chosen = jax.random.randint(key_full, (), 0, COLUMNS * BANDS)
    flat_index = jnp.arange(COLUMNS * BANDS).reshape(COLUMNS, BANDS)
    halvings = jnp.where(flat_index == chosen, 0, halvings)
    return (L_PATCH // jnp.left_shift(1, halvings)).astype(jnp.int32)


def draw_lens_region(key, part):
    position_x, position_y = lens_positions(key)
    margin = PATCH // 16
    column = jnp.arange(COLUMNS, dtype=jnp.int32).reshape(COLUMNS, 1, 1)
    band = jnp.arange(BANDS, dtype=jnp.int32).reshape(1, BANDS, 1)
    along = column * PATCH + position_x[:, :, 0, :] - margin
    along = jnp.mod(along, COLUMNS * PATCH)
    owner = along // PATCH
    stripe = along % PATCH * REG_DEV // PATCH
    spatial = (owner * BANDS + band) * REG_DEV + stripe
    labels = jax.random.permutation(jax.random.fold_in(key, 103), REGIONS).astype(jnp.int32)
    return jnp.take(labels, spatial).astype(jnp.int32)


def draw_lens_block(key, part):
    key_bins, key_factor = jax.random.split(key, 2)
    shape_kernel = (COLUMNS, BANDS, ZBINS, L_PATCH)
    lens_bin = jax.random.randint(key_bins, (COLUMNS, BANDS, 1, L_PATCH), 0, ZBINS // 2).astype(jnp.float32)
    levels = jnp.arange(ZBINS, dtype=jnp.float32).reshape(1, 1, ZBINS, 1)
    ramp_rows = jnp.maximum(levels - lens_bin, 0.0) / ZBINS
    factor = jnp.exp(jax.random.uniform(key_factor, shape_kernel, jnp.float32, -0.6931, 0.6931))
    kernel = 2.0 * ramp_rows * factor
    position_x, position_y = lens_positions(key)
    return jnp.concatenate([kernel, position_x.astype(jnp.float32), position_y.astype(jnp.float32)], axis=2).astype(jnp.bfloat16)


def bump(levels, middle, width):
    return jnp.exp(-0.5 * ((levels - middle) / width) ** 2) / (2.5066 * width)


def draw_source_block(key, part):
    key_list = jax.random.split(key, 12)
    shape_rows = (COLUMNS, BANDS, 1, S_PATCH)
    shape_pdf = (COLUMNS, BANDS, ZBINS, S_PATCH)
    center = jax.random.uniform(key_list[0], shape_rows, jnp.float32, 8.0, ZBINS - 8.0)
    spread = jax.random.uniform(key_list[1], shape_rows, jnp.float32, 2.0, 8.0)
    center_two = jax.random.uniform(key_list[8], shape_rows, jnp.float32, 4.0, ZBINS - 4.0)
    spread_two = jax.random.uniform(key_list[9], shape_rows, jnp.float32, 3.0, 10.0)
    center_wide = jax.random.uniform(key_list[10], shape_rows, jnp.float32, 0.25 * ZBINS, 0.75 * ZBINS)
    spread_wide = jax.random.uniform(key_list[11], shape_rows, jnp.float32, 20.0, 40.0)
    levels = jnp.arange(ZBINS, dtype=jnp.float32).reshape(1, 1, ZBINS, 1)
    rough_factor = jnp.exp(jax.random.uniform(key_list[2], shape_pdf, jnp.float32, -0.6931, 0.6931))
    shear_one = 0.25 * jax.random.truncated_normal(key_list[3], -3.6, 3.6, shape_rows, jnp.float32)
    shear_two = 0.25 * jax.random.truncated_normal(key_list[4], -3.6, 3.6, shape_rows, jnp.float32)
    weight = jnp.exp(jax.random.uniform(key_list[5], shape_rows, jnp.float32, math.log(0.3), math.log(3.0)))
    profile = 0.6 * bump(levels, center, spread) + 0.25 * bump(levels, center_two, spread_two)
    profile = profile + 0.1 * bump(levels, center_wide, spread_wide) + 0.05 / ZBINS
    pdf_rows = profile * rough_factor
    position_x = jax.random.randint(key_list[6], shape_rows, 0, PATCH).astype(jnp.float32)
    position_y = jax.random.randint(key_list[7], shape_rows, 0, PATCH).astype(jnp.float32)
    return jnp.concatenate([pdf_rows, position_x, position_y, shear_one, shear_two, weight], axis=2).astype(jnp.bfloat16)


def place_ends(values, own_key, low, top_value):
    longest = values.shape.index(max(values.shape))
    spots = []
    for shift in (0, 1):
        where = [jax.random.randint(jax.random.fold_in(own_key, axis), (), 0, length) for axis, length in enumerate(values.shape)]
        where[longest] = (where[longest] + shift) % values.shape[longest]
        spots.append(tuple(where))
    return values.at[spots[0]].set(low).at[spots[1]].set(top_value)


def setup_inputs(seed: int = 0) -> dict:
    arg_keys = jax.random.split(jax.random.key(seed), 6)
    lens_block = draw_lens_block(jax.random.fold_in(arg_keys[5], 71), 0)
    lens_count = draw_lens_count(jax.random.fold_in(arg_keys[5], 71), 0)
    lens_region = draw_lens_region(jax.random.fold_in(arg_keys[5], 71), 0)
    lens_sample = place_ends(jax.random.randint(arg_keys[3], (COLUMNS, BANDS, L_PATCH), 0, SAMPLES), jax.random.fold_in(arg_keys[3], 1), 0, SAMPLES - 1).astype(jnp.int32)
    source_block = draw_source_block(jax.random.fold_in(arg_keys[5], 71), 0)
    return {"lens_block": lens_block, "lens_count": lens_count, "lens_region": lens_region, "lens_sample": lens_sample, "source_block": source_block}


growth_top = 23
growth_bottom = 20

def edge_squares():
    return [float((R_IN * growth_top ** edge_level // growth_bottom ** edge_level) ** 2) for edge_level in range(NBIN + 1)]

def bin_scales():
    edge_sq = edge_squares()
    lens_per_cell = L_PATCH / (SAMPLES * REG_DEV)
    density = S_PATCH / (PATCH * PATCH)
    expected = [math.pi * (edge_sq[edge_level + 1] - edge_sq[edge_level]) * density * lens_per_cell for edge_level in range(NBIN)]
    return jnp.array(expected, jnp.float32)

def pair_sums(kernel_tile, lens_x, lens_y, source_rows, edge_sq):
    pdf_bins = kernel_tile.shape[0]
    inverse_crit = lax.dot_general(kernel_tile, source_rows[:pdf_bins], (((0,), (0,)), ((), ())), preferred_element_type=jnp.float32)
    catalog = source_rows[pdf_bins:].astype(jnp.float32)
    delta_x = catalog[0][None, :] - lens_x[:, None]
    delta_y = catalog[1][None, :] - lens_y[:, None]
    radius_sq = delta_x * delta_x + delta_y * delta_y
    safe_sq = jnp.maximum(radius_sq, edge_sq[0])
    cos_two = (delta_x * delta_x - delta_y * delta_y) / safe_sq
    sin_two = 2.0 * delta_x * delta_y / safe_sq
    tangent = -(catalog[2][None, :] * cos_two + catalog[3][None, :] * sin_two)
    weighted = catalog[4][None, :] * inverse_crit
    signal = weighted * tangent
    weight = weighted * inverse_crit
    lower_sq = jnp.array(edge_sq[:-1], jnp.float32)[:, None, None]
    upper_sq = jnp.array(edge_sq[1:], jnp.float32)[:, None, None]
    inside = (radius_sq[None] >= lower_sq) & (radius_sq[None] < upper_sq)
    signal_bins = lax.optimization_barrier(jnp.sum(jnp.where(inside, signal[None], 0.0), axis=2))
    weight_bins = lax.optimization_barrier(jnp.sum(jnp.where(inside, weight[None], 0.0), axis=2))
    return jnp.stack([signal_bins, weight_bins], axis=0)

def local_terms(lens_tile, neighbours, edge_sq):
    pdf_bins = lens_tile.shape[0] - 2
    kernel_tile = lens_tile[:pdf_bins]
    lens_x = lens_tile[pdf_bins].astype(jnp.float32)
    lens_y = lens_tile[pdf_bins + 1].astype(jnp.float32)
    totals = jnp.zeros((2, len(edge_sq) - 1, lens_tile.shape[1]), jnp.float32)
    for shift_x in (-1, 0, 1):
        for shift_y in (-1, 0, 1):
            source_rows = neighbours[3 * (shift_x + 1) + shift_y + 1]
            totals = totals + pair_sums(kernel_tile, lens_x - shift_x * PATCH, lens_y - shift_y * PATCH, source_rows, edge_sq)
    return totals

def reference(lens_block, lens_count, lens_region, lens_sample, source_block):
    edge_sq = edge_squares()
    padded = jnp.pad(source_block, ((0, 0), (1, 1), (0, 0), (0, 0)))
    tile_rows = math.gcd(L_PATCH, 128)
    starts = jnp.arange(L_PATCH // tile_rows, dtype=jnp.int32) * tile_rows

    def patch_terms(patch_index):
        column = patch_index // BANDS
        row_index = patch_index % BANDS
        lenses = lens_block[column, row_index]
        neighbours = []
        for shift_x in (-1, 0, 1):
            for shift_y in (-1, 0, 1):
                neighbours.append(padded[(column + shift_x) % COLUMNS, row_index + 1 + shift_y])

        def tile_terms(first_lens):
            lens_tile = lax.dynamic_slice_in_dim(lenses, first_lens, tile_rows, 1)
            return local_terms(lens_tile, neighbours, edge_sq)
        pieces = lax.map(tile_terms, starts)
        totals = jnp.transpose(pieces, (1, 2, 0, 3)).reshape(2, NBIN, L_PATCH)
        live_lens = jnp.arange(L_PATCH, dtype=jnp.int32) < lens_count[column, row_index]
        return jnp.where(live_lens[None, None, :], totals, 0.0)
    per_patch = lax.map(patch_terms, jnp.arange(COLUMNS * BANDS, dtype=jnp.int32))
    per_lens = jnp.transpose(per_patch, (0, 3, 1, 2)).reshape(COLUMNS * BANDS * L_PATCH, 2 * NBIN)
    segment = (lens_region * SAMPLES + lens_sample).reshape(-1).astype(jnp.int32)
    region_table = jax.ops.segment_sum(per_lens, segment, num_segments=REGIONS * SAMPLES)
    region_table = region_table.reshape(REGIONS, SAMPLES, 2, NBIN)
    scales = bin_scales()
    return (region_table[:, :, 0, :] / jnp.sqrt(scales), region_table[:, :, 1, :] / scales)
```

```python
import functools
import math

import jax
import jax.numpy as jnp
import numpy as np
from jax import lax
from jax.experimental import pallas as pl
from jax.experimental.pallas import tpu as pltpu
from jax.sharding import PartitionSpec as P

NBIN = 20
SAMPLES = 8
PATCH = 256
R_IN = 12
L_PATCH = 512
S_PATCH = 1024
REG_DEV = 8
ZROWS = 128
LANES = 128
SUB = 8
SRC_TILES = S_PATCH // LANES
LENS_TILES = L_PATCH // SUB
UNROLL = 4
FAR = 1.0e6
BOX_ROW = ZROWS + 5
BLOCK_ROWS = 144
COUNT_LANE = 120
FOLD = 2
VMEM_MIB = 40
THRESHOLD_SUMS = 2 * (NBIN + 1)
growth_top = 23
growth_bottom = 20


def edge_squares():
    return [
        float((R_IN * growth_top**k // growth_bottom**k) ** 2) for k in range(NBIN + 1)
    ]


EDGES = edge_squares()
GROUPS = ((0, 10), (10, 16), (16, 21))


def bin_scales():
    lens_per_cell = L_PATCH / (SAMPLES * REG_DEV)
    density = S_PATCH / (PATCH * PATCH)
    expected = [
        math.pi * (EDGES[k + 1] - EDGES[k]) * density * lens_per_cell for k in range(NBIN)
    ]
    return jnp.array(expected, jnp.float32)


def tree_sum(terms):
    while len(terms) > 1:
        paired = [a + b for a, b in zip(terms[::2], terms[1::2])]
        terms = paired + ([terms[-1]] if len(terms) % 2 else [])
    return terms[0]


def spatial_order(x, y, dead, group):
    n = x.shape[0]
    index = jnp.arange(n, dtype=jnp.float32)
    key = x * n + index + dead * 2.0**20
    rank = jnp.sum((key[:, None] < key[None, :]).astype(jnp.float32), axis=0)
    key = jnp.floor(rank / group) * 2.0**18 + y * n + index
    return jnp.sum((key[:, None] < key[None, :]).astype(jnp.float32), axis=0)


def order_matrix(rank):
    n = rank.shape[0]
    target = lax.broadcasted_iota(jnp.float32, (n, n), 0)
    return (target == rank[None, :]).astype(jnp.bfloat16)


def tile_boxes(x, y):
    x, y = x.reshape(-1, LANES), y.reshape(-1, LANES)
    return jnp.stack([jnp.min(x, 1), jnp.max(x, 1), jnp.min(y, 1), jnp.max(y, 1)])


def tile_lists(columns_ref, boxes, valid, tiles, slots):
    wide = (LENS_TILES, LANES)

    def bound(row, reduce):
        column = columns_ref[:, ZROWS + row : ZROWS + row + 1]
        return reduce(column.reshape(LENS_TILES, SUB, 1), axis=1)

    gap_x = jnp.maximum(boxes[0] - bound(0, jnp.max), bound(0, jnp.min) - boxes[1])
    gap_y = jnp.maximum(boxes[2] - bound(1, jnp.max), bound(1, jnp.min) - boxes[3])
    gap_x, gap_y = jnp.maximum(gap_x, 0.0), jnp.maximum(gap_y, 0.0)
    near_sq = jnp.where(valid, gap_x * gap_x + gap_y * gap_y, FAR)
    upper = (
        (lax.broadcasted_iota(jnp.int32, (LANES, LANES), 0)
        <= lax.broadcasted_iota(jnp.int32, (LANES, LANES), 1)).astype(jnp.float32)
    ).astype(jnp.bfloat16)
    lane = lax.broadcasted_iota(jnp.int32, wide, 1)
    tile_id = lane.astype(jnp.float32) - tiles
    place = jnp.full(wide, -1.0, jnp.float32)
    base = jnp.zeros((LENS_TILES, 1), jnp.float32)
    listed = jnp.zeros(wide, jnp.float32)
    inner = jnp.zeros(wide, jnp.float32)
    for group, (_, hi) in enumerate(GROUPS):
        reach = (near_sq < EDGES[hi - 1]).astype(jnp.float32)
        member = reach - inner
        inner = reach
        running = jnp.dot(
            member.astype(jnp.bfloat16), upper, preferred_element_type=jnp.float32
        )
        place = jnp.where(member > 0.0, running + (base - 1.0), place)
        base = base + running[:, LANES - 1 :]
        listed = jnp.where(lane == COUNT_LANE + group, base - tiles, listed)
    for slot in range(slots):
        found = jnp.sum(jnp.where(place == float(slot), tile_id, 0.0), axis=1, keepdims=True)
        listed = jnp.where(lane == slot, found, listed)
    return (listed + tiles).astype(jnp.int32)


def pair_kernel(shifts, last, *refs):
    n = sum(len(group) for group in shifts)
    tiles = n * SRC_TILES
    live_ref, band_ref, columns_ref = refs[:3]
    blocks = refs[3 : 3 + len(shifts)]
    rest = refs[3 + len(shifts) :]
    if last:
        before_ref, out_ref, sums, *rest = rest
    else:
        before_ref, (sums, *rest) = None, rest
    crit, param, slots, list_vmem, list_ref, list_sem = rest
    live = live_ref[0]
    tile_shape = (SUB, LANES)
    patches = [
        (block, at, shift)
        for block, group in zip(blocks, shifts)
        for at, shift in enumerate(group)
    ]

    lane = lax.broadcasted_iota(jnp.int32, (1, LANES), 1)
    boxes = [jnp.zeros((1, LANES), jnp.float32) for _ in range(4)]
    valid = jnp.zeros((1, LANES), jnp.float32)
    for p, (block, at, shift) in enumerate(patches):
        own = (lane >= p * SRC_TILES) & (lane < (p + 1) * SRC_TILES)
        rows = block[at, BOX_ROW : BOX_ROW + 4, :LANES].astype(jnp.float32)
        rows = pltpu.roll(rows, p * SRC_TILES, axis=1)
        for c in range(4):
            boxes[c] = jnp.where(own, rows[c : c + 1] + shift[c // 2] * PATCH, boxes[c])
        there = band_ref[0] + shift[1]
        inside = ((there >= 0) & (there < band_ref[1])).astype(jnp.float32)
        valid = jnp.where(own, inside, valid)
    list_vmem[...] = tile_lists(
        columns_ref, boxes, valid > 0.0, tiles, -(-tiles // UNROLL) * UNROLL
    )
    copy = pltpu.make_async_copy(list_vmem, list_ref, list_sem)
    copy.start()

    for p, (block, at, (shift_x, shift_y)) in enumerate(patches):
        rows = block[at, ZROWS : ZROWS + 5, :].astype(jnp.float32)
        weight = rows[4:5]
        values = (
            rows[0:1] + shift_x * PATCH,
            rows[1:2] + shift_y * PATCH,
            -(weight * rows[2:3]),
            -2.0 * (weight * rows[3:4]),
            weight,
        )
        for t in range(SRC_TILES):
            for v, value in enumerate(values):
                param[p * SRC_TILES + t, v] = jnp.broadcast_to(
                    value[:, t * LANES : (t + 1) * LANES], tile_shape
                )
    for v in range(5):
        param[tiles, v] = jnp.full(tile_shape, FAR if v == 0 else 0.0, jnp.float32)
    crit[tiles] = jnp.zeros((L_PATCH, LANES), jnp.float32)

    def crit_step(chunk, carry):
        first = pl.multiple_of(chunk * LANES, LANES)
        kernel_rows = columns_ref[pl.ds(first, LANES), :ZROWS].astype(jnp.bfloat16)
        for p, (block, at, _) in enumerate(patches):
            product = jnp.dot(
                kernel_rows, block[at, :ZROWS, :], preferred_element_type=jnp.float32
            )
            for t in range(SRC_TILES):
                crit[p * SRC_TILES + t, pl.ds(first, LANES), :] = product[
                    :, t * LANES : (t + 1) * LANES
                ]
        return carry

    lax.fori_loop(0, (live + LANES - 1) // LANES, crit_step, 0)
    copy.wait()

    def gather(terms, carry, group):
        lo, hi = GROUPS[group]
        out = []
        for k in range(lo, hi):
            inside = [r2 < EDGES[k] for _, _, r2 in terms]
            for c in range(2):
                picked = [jnp.where(m, t[c], 0.0) for m, t in zip(inside, terms)]
                out.append(carry[2 * (k - lo) + c] + tree_sum(picked))
        return tuple(out)

    def lens_step(lens_tile, carry):
        first = pl.multiple_of(lens_tile * SUB, SUB)
        place = columns_ref[pl.ds(first, SUB), ZROWS : ZROWS + 2]
        lens_x = jnp.broadcast_to(place[:, 0:1], tile_shape)
        lens_y = jnp.broadcast_to(place[:, 1:2], tile_shape)

        def far_step(i, acc):
            terms = []
            for u in range(UNROLL):
                tile = list_ref[lens_tile, i * UNROLL + u]
                dx = param[tile, 0] - lens_x
                dy = param[tile, 1] - lens_y
                dx_sq, dy_sq = dx * dx, dy * dy
                r2 = dx_sq + dy_sq
                turned = param[tile, 2] * (dx_sq - dy_sq) + param[tile, 3] * (dx * dy)
                value = crit[tile, pl.ds(first, SUB), :]
                signal = value * (turned / jnp.maximum(r2, EDGES[0]))
                weight = param[tile, 4] * value * value
                slots[0, i * UNROLL + u] = signal
                slots[1, i * UNROLL + u] = weight
                slots[2, i * UNROLL + u] = r2
                terms.append((signal, weight, r2))
            return gather(terms, acc, 2)

        def near_step(group, i, acc):
            terms = [
                tuple(slots[c, i * UNROLL + u] for c in range(3)) for u in range(UNROLL)
            ]
            return gather(terms, acc, group)

        for group in (2, 1, 0):
            step = far_step if group == 2 else functools.partial(near_step, group)
            trips = (list_ref[lens_tile, COUNT_LANE + group] + UNROLL - 1) // UNROLL
            places = [
                c * (NBIN + 1) + k for k in range(*GROUPS[group]) for c in range(2)
            ]
            if before_ref is None:
                acc = (jnp.zeros(tile_shape, jnp.float32),) * len(places)
            else:
                acc = tuple(before_ref[lens_tile, v] for v in places)
            acc = lax.fori_loop(0, trips, step, acc)
            for v, value in zip(places, acc):
                sums[lens_tile, v] = value
        return carry

    lens_tiles = live // SUB
    lax.fori_loop(0, lens_tiles, lens_step, 0)

    if not last:
        return
    out_ref[...] = jnp.zeros_like(out_ref)

    lane = lax.broadcasted_iota(jnp.int32, tile_shape, 1)
    ones = jnp.ones((2 * LANES, LANES), jnp.bfloat16)

    def fold_step(step, carry):
        rows = (NBIN + 1) * SUB
        for u in range(FOLD):
            tile = step * FOLD + u
            total = jnp.zeros(tile_shape, jnp.float32)
            value = sums[tile, NBIN + 1 :].reshape(rows, LANES)
            high = value.astype(jnp.bfloat16)
            low = (value - high.astype(jnp.float32)).astype(jnp.bfloat16)
            both = jnp.concatenate([high, low], axis=1)
            folded = jnp.dot(both, ones, preferred_element_type=jnp.float32)
            for k in range(NBIN + 1):
                signal = jnp.sum(sums[tile, k], axis=1, keepdims=True)
                total = jnp.where(lane == k, signal, total)
                weight = folded[k * SUB : (k + 1) * SUB]
                total = jnp.where(lane == NBIN + 1 + k, weight, total)
            out_ref[pl.ds(pl.multiple_of(tile * SUB, SUB), SUB), :] = total
        return carry

    lax.fori_loop(0, lens_tiles // FOLD, fold_step, 0)


def pair_sums(live, bands, columns, blocks, shifts, before=None):
    n = sum(len(group) for group in shifts)
    tiles = n * SRC_TILES
    padded = -(-tiles // UNROLL) * UNROLL
    last = before is not None
    smem = pl.BlockSpec(memory_space=pltpu.SMEM)
    vmem = pl.BlockSpec(memory_space=pltpu.VMEM)
    all_sums = (LENS_TILES, THRESHOLD_SUMS, SUB, LANES)
    scratch = [
        pltpu.VMEM((tiles + 1, L_PATCH, LANES), jnp.float32),
        pltpu.VMEM((tiles + 1, 5, SUB, LANES), jnp.float32),
        pltpu.VMEM((3, padded, SUB, LANES), jnp.float32),
        pltpu.VMEM((LENS_TILES, LANES), jnp.int32),
        pltpu.SMEM((LENS_TILES, LANES), jnp.int32),
        pltpu.SemaphoreType.DMA,
    ]
    operands = (live, bands, columns, *blocks) + ((before,) if last else ())
    return pl.pallas_call(
        functools.partial(pair_kernel, shifts, last),
        out_shape=jax.ShapeDtypeStruct((L_PATCH, LANES) if last else all_sums, jnp.float32),
        in_specs=[smem] * 2 + [vmem] * (len(operands) - 2),
        out_specs=vmem,
        scratch_shapes=([pltpu.VMEM(all_sums, jnp.float32)] if last else []) + scratch,
        cost_estimate=pl.CostEstimate(
            flops=n * 20_000_000_000, transcendentals=0, bytes_accessed=n * 300_000
        ),
        compiler_params=pltpu.CompilerParams(vmem_limit_bytes=VMEM_MIB << 20),
        name=f"pairs_{n}",
    )(*operands)


WIDE = 3 * LANES


def split_parts(value):
    parts = []
    for _ in range(3):
        part = value.astype(jnp.bfloat16)
        value = value - part.astype(jnp.float32)
        parts.append(part)
    return parts


def bin_placement():
    matrix = np.zeros((LANES, WIDE), np.float32)
    for m in range(SAMPLES):
        for c in range(2):
            for k in range(NBIN):
                column = (m * 2 + c) * NBIN + k
                matrix[c * (NBIN + 1) + k + 1, column] = 1.0
                matrix[c * (NBIN + 1) + k, column] = -1.0
    return jnp.asarray(matrix, jnp.bfloat16)


def table_kernel(rows_ref, columns_ref, sums_ref, place_ref, out_ref):
    place = place_ref[...]
    parts = split_parts(sums_ref[...])
    bins = [jnp.dot(p, place, preferred_element_type=jnp.float32) for p in parts]
    bins = (bins[2] + bins[1]) + bins[0]
    sample = columns_ref[:, ZROWS + 4 : ZROWS + 5].astype(jnp.int32) * (2 * NBIN)
    lane = lax.broadcasted_iota(jnp.int32, bins.shape, 1) - sample
    bins = jnp.where((lane >= 0) & (lane < 2 * NBIN), bins, 0.0)
    region = (rows_ref[2:3] * 8.0 + rows_ref[3:4]).astype(jnp.int32)
    ids = lax.broadcasted_iota(jnp.int32, (out_ref.shape[0], region.shape[1]), 0)
    match = (ids == region).astype(jnp.float32).astype(jnp.bfloat16)
    sums = [jnp.dot(match, p, preferred_element_type=jnp.float32) for p in split_parts(bins)]
    out_ref[...] = (sums[2] + sums[1]) + sums[0]


def region_sums(rows, columns, per_lens, regions_total):
    vmem = pl.BlockSpec(memory_space=pltpu.VMEM)
    return pl.pallas_call(
        table_kernel,
        out_shape=jax.ShapeDtypeStruct((regions_total, WIDE), jnp.float32),
        in_specs=[vmem] * 4,
        out_specs=vmem,
        compiler_params=pltpu.CompilerParams(vmem_limit_bytes=32 << 20),
        name="region_table",
    )(rows, columns, per_lens, bin_placement())


def shifted(block, axis, periodic):
    count = lax.axis_size(axis)
    forward = [(i, i + 1) for i in range(count - 1)]
    if periodic:
        forward.append((count - 1, 0))
    backward = [(b, a) for a, b in forward]
    return lax.ppermute(block, axis, forward), lax.ppermute(block, axis, backward)


def on_device(lens_block, lens_count, lens_region, lens_sample, source_block):
    axes = ("ra", "dec")
    bands, band = lax.axis_size("dec"), lax.axis_index("dec")
    regions_total = REG_DEV * lax.axis_size("ra") * bands
    nothing = (((1,), (1,)), ((), ()))

    source = source_block[0, 0]
    source_rank = spatial_order(
        source[ZROWS].astype(jnp.float32), source[ZROWS + 1].astype(jnp.float32), 0.0, 256
    )
    source = lax.dot_general(
        source, order_matrix(source_rank), nothing, preferred_element_type=jnp.float32
    )
    boxes = tile_boxes(source[ZROWS], source[ZROWS + 1])
    boxes = jnp.pad(boxes, ((0, BLOCK_ROWS - BOX_ROW - 4), (0, S_PATCH - SRC_TILES)))
    source = jnp.concatenate([source, boxes], axis=0).astype(jnp.bfloat16)

    low, high = shifted(source, "ra", True)
    middle = jnp.stack([source, low, high])
    columns_at = (0, -1, 1)
    with jax.named_scope("halo_dec"):
        below, above = shifted(middle, "dec", False)

    lens = lens_block[0, 0]
    live = lens_count[0]
    dead = (jnp.arange(L_PATCH, dtype=jnp.int32) >= live[0]).astype(jnp.float32)
    lens_rank = spatial_order(
        lens[ZROWS].astype(jnp.float32), lens[ZROWS + 1].astype(jnp.float32), dead, 64
    )
    order = order_matrix(lens_rank)
    region, sample = lens_region[0], lens_sample[0]
    labels = jnp.concatenate([region // 8, region % 8, sample], axis=0).astype(jnp.bfloat16)
    lens = jnp.concatenate([lens, labels], axis=0)
    columns = lax.dot_general(order, lens, nothing, preferred_element_type=jnp.float32)
    rows = lax.dot_general(lens[ZROWS:], order, nothing, preferred_element_type=jnp.float32)
    where = jnp.stack([band, jnp.int32(bands)]).astype(jnp.int32)

    with jax.named_scope("pairs_near"):
        shifts = (tuple((a, 0) for a in columns_at),)
        near = pair_sums(live, where, columns, [middle], shifts)
    with jax.named_scope("pairs_far"):
        shifts = tuple(tuple((a, b) for a in columns_at) for b in (-1, 1))
        per_lens = pair_sums(live, where, columns, [below, above], shifts, near)

    table = region_sums(rows, columns, per_lens, regions_total)
    table = lax.all_to_all(table, axes, 0, 0, tiled=True)
    owned = jnp.sum(table.reshape(-1, REG_DEV, WIDE), axis=0)
    owned = owned[:, : 2 * NBIN * SAMPLES].reshape(REG_DEV, SAMPLES, 2, NBIN)
    scales = bin_scales()
    return (owned[:, :, 0, :] / jnp.sqrt(scales), owned[:, :, 1, :] / scales)


def solution(mesh):
    placed = (
        P("ra", "dec", None, None),
        P("ra", "dec"),
        P("ra", "dec", None),
        P("ra", "dec", None),
        P("ra", "dec", None, None),
    )
    return jax.shard_map(
        on_device,
        mesh=mesh,
        in_specs=placed,
        out_specs=(P(("ra", "dec"), None, None), P(("ra", "dec"), None, None)),
        check_vma=False,
    )
```

```python
import functools
import math

import jax
import jax.numpy as jnp
import numpy as np
from jax import lax
from jax.experimental import pallas as pl
from jax.experimental.pallas import tpu as pltpu
from jax.sharding import PartitionSpec as P

NBIN = 20
SAMPLES = 8
PATCH = 256
R_IN = 12
L_PATCH = 512
S_PATCH = 1024
REG_DEV = 8
ZROWS = 128
LANES = 128
SUB = 8
SRC_TILES = S_PATCH // LANES
LENS_TILES = L_PATCH // SUB
UNROLL = (4, 4, 4)
CRIT_ROW = 5 * SUB
FAR = 1.0e6
BOX_ROW = ZROWS + SUB
BLOCK_ROWS = 144
LIST_WORDS = 16
FOLD_SPLIT = 22
VMEM_MIB = 26
THRESHOLD_SUMS = 2 * (NBIN + 1)
WIDE = 3 * LANES
growth_top = 23
growth_bottom = 20


def edge_squares():
    return [
        float((R_IN * growth_top**k // growth_bottom**k) ** 2) for k in range(NBIN + 1)
    ]


EDGES = edge_squares()
GROUPS = ((0, 10), (10, 16), (16, 21))


def bin_scales():
    lens_per_cell = L_PATCH / (SAMPLES * REG_DEV)
    density = S_PATCH / (PATCH * PATCH)
    expected = [
        math.pi * (EDGES[k + 1] - EDGES[k]) * density * lens_per_cell for k in range(NBIN)
    ]
    return jnp.array(expected, jnp.float32)


def tree_sum(terms):
    while len(terms) > 1:
        paired = [a + b for a, b in zip(terms[::2], terms[1::2])]
        terms = paired + ([terms[-1]] if len(terms) % 2 else [])
    return terms[0]


def spatial_order(x, y, dead, group):
    n = x.shape[0]
    index = jnp.arange(n, dtype=jnp.float32)
    key = x * n + index + dead * 2.0**20
    rank = jnp.sum((key[:, None] < key[None, :]).astype(jnp.float32), axis=0)
    key = jnp.floor(rank / group) * 2.0**18 + y * n + index
    return jnp.sum((key[:, None] < key[None, :]).astype(jnp.float32), axis=0)


def order_matrix(rank):
    n = rank.shape[0]
    target = lax.broadcasted_iota(jnp.float32, (n, n), 0)
    return (target == rank[None, :]).astype(jnp.bfloat16)


def tile_boxes(x, y):
    x, y = x.reshape(-1, LANES), y.reshape(-1, LANES)
    return jnp.stack([jnp.min(x, 1), jnp.max(x, 1), jnp.min(y, 1), jnp.max(y, 1)])


def tile_lists(lens_box, boxes, valid, tiles):
    wide = (tiles, LANES)
    gap_x = jnp.maximum(boxes[0] - lens_box[1:2], lens_box[0:1] - boxes[1])
    gap_y = jnp.maximum(boxes[2] - lens_box[3:4], lens_box[2:3] - boxes[3])
    gap_x, gap_y = jnp.maximum(gap_x, 0.0), jnp.maximum(gap_y, 0.0)
    near_sq = jnp.where(valid, gap_x * gap_x + gap_y * gap_y, FAR)
    lower = lax.broadcasted_iota(jnp.int32, (tiles, tiles), 0)
    lower = (lower >= lax.broadcasted_iota(jnp.int32, (tiles, tiles), 1)).astype(jnp.float32)
    lower = lower.astype(jnp.bfloat16)
    tile_id = lax.broadcasted_iota(jnp.int32, wide, 0).astype(jnp.float32) - tiles
    place = jnp.full(wide, -1.0, jnp.float32)
    base = jnp.zeros((1, LANES), jnp.float32)
    inner = jnp.zeros(wide, jnp.float32)
    trips = []
    for group, (_, hi) in enumerate(GROUPS):
        reach = (near_sq < EDGES[hi - 1]).astype(jnp.float32)
        member = (reach - inner).astype(jnp.bfloat16)
        running = jnp.dot(lower, member, preferred_element_type=jnp.float32)
        place = jnp.where(reach > inner, running + (base - 1.0), place)
        inner = reach
        base = base + running[tiles - 1 :]
        trips.append(jnp.floor((base + (UNROLL[group] - 1)) * (1.0 / UNROLL[group])))
    partial = []
    for slot in range(tiles):
        hit = jnp.where(place == float(slot), tile_id, 0.0)
        partial.append(tree_sum([hit[r : r + SUB] for r in range(0, tiles, SUB)]))
    partial = jnp.concatenate(partial, axis=0).astype(jnp.bfloat16)
    words = LIST_WORDS
    row = lax.broadcasted_iota(jnp.int32, (2 * words, tiles * SUB), 0)
    slot = lax.broadcasted_iota(jnp.int32, (2 * words, tiles * SUB), 1) >> 3
    first = 4 * (row & (words - 1)) + 2 * (row >> 4)
    take = jnp.where(slot == first, 1.0, jnp.where(slot == first + 1, 128.0, 0.0))
    packed = jnp.dot(take.astype(jnp.bfloat16), partial, preferred_element_type=jnp.float32)
    packed = (packed + 129.0 * tiles).astype(jnp.int32)
    packed = packed[:words] + packed[words:] * (1 << 14)
    row = lax.broadcasted_iota(jnp.int32, (SUB, LANES), 0)
    counts = jnp.where(row == 0, trips[0], jnp.where(row == 1, trips[1], trips[2]))
    return jnp.concatenate([packed, counts.astype(jnp.int32)], axis=0)


def pair_kernel(shifts, later, last, *refs):
    n = sum(len(group) for group in shifts)
    tiles = n * SRC_TILES
    live_ref, band_ref, columns_ref, place_ref, box_ref = refs[:5]
    blocks = refs[5 : 5 + len(shifts)]
    rest = refs[5 + len(shifts) :]
    before_ref = None
    if later:
        before_ref, *rest = rest
    if last:
        fold_ref, out_ref, *rest = rest
    sums, *rest = rest
    tables, slots, list_vmem, list_ref, list_sem = rest
    live = live_ref[0]
    tile_shape = (SUB, LANES)
    patches = [
        (block, at, shift)
        for block, group in zip(blocks, shifts)
        for at, shift in enumerate(group)
    ]

    boxes, valid = [[] for _ in range(4)], []
    for block, at, shift in patches:
        for c in range(4):
            part = block[at, BOX_ROW : BOX_ROW + SUB, c * LANES : (c + 1) * LANES]
            boxes[c].append(part.astype(jnp.float32) + shift[c // 2] * PATCH)
        there = band_ref[0] + shift[1]
        inside = (there >= 0) & (there < band_ref[1])
        valid.append(jnp.full(tile_shape, inside.astype(jnp.float32)))
    boxes = [jnp.concatenate(box, axis=0) for box in boxes]
    valid = jnp.concatenate(valid, axis=0) > 0.0
    list_vmem[...] = tile_lists(box_ref[...], boxes, valid, tiles)
    copy = pltpu.make_async_copy(list_vmem, list_ref, list_sem)
    copy.start()

    for p, (block, at, (shift_x, shift_y)) in enumerate(patches):
        rows = block[at, ZROWS : ZROWS + 5, :].astype(jnp.float32)
        weight = rows[4:5]
        values = (
            rows[0:1] + shift_x * PATCH,
            rows[1:2] + shift_y * PATCH,
            -(weight * rows[2:3]),
            -2.0 * (weight * rows[3:4]),
            weight,
        )
        for t in range(SRC_TILES):
            for v, value in enumerate(values):
                tables[p * SRC_TILES + t, v * SUB : (v + 1) * SUB] = jnp.broadcast_to(
                    value[:, t * LANES : (t + 1) * LANES], tile_shape
                )
    for v in range(5):
        tables[tiles, v * SUB : (v + 1) * SUB] = jnp.full(
            tile_shape, FAR if v == 0 else 0.0, jnp.float32
        )
    tables[tiles, CRIT_ROW:] = jnp.zeros((L_PATCH, LANES), jnp.float32)

    def crit_step(chunk, carry):
        first = pl.multiple_of(chunk * LANES, LANES)
        kernel_rows = columns_ref[pl.ds(first, LANES), :ZROWS].astype(jnp.bfloat16)
        for p, (block, at, _) in enumerate(patches):
            product = jnp.dot(
                kernel_rows, block[at, :ZROWS, :], preferred_element_type=jnp.float32
            )
            for t in range(SRC_TILES):
                tables[p * SRC_TILES + t, pl.ds(CRIT_ROW + first, LANES), :] = product[
                    :, t * LANES : (t + 1) * LANES
                ]
        return carry

    lax.fori_loop(0, (live + LANES - 1) // LANES, crit_step, 0)
    copy.wait()

    def add_up(rows, terms, group):
        for k in range(*GROUPS[group]):
            inside = [r2 < EDGES[k] for _, _, r2 in terms]
            for c in range(2):
                picked = [jnp.where(m, t[c], 0.0) for m, t in zip(inside, terms)]
                at = c * (NBIN + 1) + k
                sums[at, rows, :] = sums[at, rows, :] + tree_sum(picked)

    def lens_step(lens_tile, base):
        first = pl.multiple_of(lens_tile * SUB, SUB)
        rows = pl.ds(pl.multiple_of(first - base, SUB), SUB)
        trips = [list_ref[LIST_WORDS + group, lens_tile] for group in range(3)]
        lens_x = place_ref[0, pl.ds(first, SUB), :]
        lens_y = place_ref[1, pl.ds(first, SUB), :]
        for v in range(THRESHOLD_SUMS):
            sums[v, rows, :] = (
                before_ref[v, pl.ds(first, SUB), :] if later else jnp.zeros(tile_shape, jnp.float32)
            )

        def far_step(i, word):
            following = list_ref[i + 1, lens_tile]
            terms = []
            for u in range(4):
                tile = (word >> (7 * u)) & 127
                dx, dy = tables[tile, 0:SUB] - lens_x, tables[tile, SUB : 2 * SUB] - lens_y
                dx_sq, dy_sq = dx * dx, dy * dy
                r2 = dx_sq + dy_sq
                turned = tables[tile, 2 * SUB : 3 * SUB] * (dx_sq - dy_sq)
                turned = turned + tables[tile, 3 * SUB : 4 * SUB] * (dx * dy)
                value = tables[tile, pl.ds(CRIT_ROW + first, SUB), :]
                signal = value * (turned / jnp.maximum(r2, EDGES[0]))
                weight = tables[tile, 4 * SUB : 5 * SUB] * value * value
                slots[0, i * UNROLL[2] + u] = signal
                slots[1, i * UNROLL[2] + u] = weight
                slots[2, i * UNROLL[2] + u] = r2
                terms.append((signal, weight, r2))
            add_up(rows, terms, 2)
            return following

        lax.fori_loop(0, trips[2], far_step, list_ref[0, lens_tile])
        for group in (1, 0):

            def near_step(i, nothing, group=group):
                terms = [
                    tuple(slots[c, i * UNROLL[group] + u] for c in range(3))
                    for u in range(UNROLL[group])
                ]
                add_up(rows, terms, group)
                return nothing

            lax.fori_loop(0, trips[group], near_step, 0)
        return base

    lens_tiles = live // SUB
    if not last:
        lax.fori_loop(0, lens_tiles, lens_step, 0)
        return
    out_ref[...] = jnp.zeros_like(out_ref)

    def chunk_step(chunk, carry):
        first = pl.multiple_of(chunk * LANES, LANES)
        tiles_first = chunk * (LANES // SUB)
        tiles_end = jnp.minimum(tiles_first + LANES // SUB, lens_tiles)
        lax.fori_loop(tiles_first, tiles_end, lens_step, first)
        high, low = [], []
        for v in range(THRESHOLD_SUMS):
            value = sums[v]
            high.append(value.astype(jnp.bfloat16))
            low.append((value - high[v].astype(jnp.float32)).astype(jnp.bfloat16))
        folded = []
        for lo, hi in ((0, FOLD_SPLIT), (FOLD_SPLIT, THRESHOLD_SUMS)):
            both = [jnp.concatenate(part[lo:hi], axis=1) for part in (high, low)]
            weights = fold_ref[lo * LANES : hi * LANES, :]
            folded += [jnp.dot(p, weights, preferred_element_type=jnp.float32) for p in both]
        folded = tree_sum(folded)
        row = lax.broadcasted_iota(jnp.int32, (LANES, LANES), 0) + first
        folded = jnp.where(row < live, folded, 0.0)
        out_ref[pl.ds(first, LANES), :] = folded
        return carry

    lax.fori_loop(0, (live + LANES - 1) // LANES, chunk_step, 0)


def fold_matrix():
    matrix = np.zeros((THRESHOLD_SUMS, LANES, LANES), np.float32)
    for v in range(THRESHOLD_SUMS):
        matrix[v, :, v] = 1.0
    return jnp.asarray(matrix.reshape(-1, LANES), jnp.bfloat16)


def pair_sums(live, bands, columns, place, lens_box, blocks, shifts, before=None, last=False):
    n = sum(len(group) for group in shifts)
    tiles = n * SRC_TILES
    later = before is not None
    smem = pl.BlockSpec(memory_space=pltpu.SMEM)
    vmem = pl.BlockSpec(memory_space=pltpu.VMEM)
    all_sums = (THRESHOLD_SUMS, L_PATCH, LANES)
    scratch = [
        pltpu.VMEM((tiles + 1, CRIT_ROW + L_PATCH, LANES), jnp.float32),
        pltpu.VMEM((3, tiles, SUB, LANES), jnp.float32),
        pltpu.VMEM((LIST_WORDS + SUB, LANES), jnp.int32),
        pltpu.SMEM((LIST_WORDS + SUB, LANES), jnp.int32),
        pltpu.SemaphoreType.DMA,
    ]
    operands = (live, bands, columns, place, lens_box, *blocks)
    operands += (before,) if later else ()
    operands += (fold_matrix(),) if last else ()
    return pl.pallas_call(
        functools.partial(pair_kernel, shifts, later, last),
        out_shape=jax.ShapeDtypeStruct((L_PATCH, LANES) if last else all_sums, jnp.float32),
        in_specs=[smem] * 2 + [vmem] * (len(operands) - 2),
        out_specs=vmem,
        input_output_aliases={5 + len(blocks): 0} if later and not last else {},
        scratch_shapes=([pltpu.VMEM((THRESHOLD_SUMS, LANES, LANES), jnp.float32)] if last else []) + scratch,
        cost_estimate=pl.CostEstimate(
            flops=n * 20_000_000_000, transcendentals=0, bytes_accessed=n * 300_000
        ),
        compiler_params=pltpu.CompilerParams(vmem_limit_bytes=VMEM_MIB << 20),
        name=f"pairs_{n}",
    )(*operands)


def split_parts(value):
    parts = []
    for _ in range(3):
        part = value.astype(jnp.bfloat16)
        value = value - part.astype(jnp.float32)
        parts.append(part)
    return parts


def bin_placement():
    matrix = np.zeros((LANES, WIDE), np.float32)
    for m in range(SAMPLES):
        for c in range(2):
            for k in range(NBIN):
                column = (m * 2 + c) * NBIN + k
                matrix[c * (NBIN + 1) + k + 1, column] = 1.0
                matrix[c * (NBIN + 1) + k, column] = -1.0
    return jnp.asarray(matrix, jnp.bfloat16)


def table_kernel(region_ref, sample_ref, sums_ref, place_ref, out_ref):
    def product(matrices, others):
        terms = [
            jnp.dot(a, b, preferred_element_type=jnp.float32) for a, b in zip(matrices, others)
        ]
        return (terms[2] + terms[1]) + terms[0]

    bins = product(split_parts(sums_ref[...]), [place_ref[...]] * 3)
    lane = lax.broadcasted_iota(jnp.int32, bins.shape, 1) - sample_ref[...] * (2 * NBIN)
    bins = jnp.where((lane >= 0) & (lane < 2 * NBIN), bins, 0.0)
    region = region_ref[...]
    ids = lax.broadcasted_iota(jnp.int32, (out_ref.shape[0], region.shape[1]), 0)
    match = (ids == region).astype(jnp.float32).astype(jnp.bfloat16)
    out_ref[...] = product([match] * 3, split_parts(bins))


def region_sums(region, sample, sums, regions_total):
    vmem = pl.BlockSpec(memory_space=pltpu.VMEM)
    return pl.pallas_call(
        table_kernel,
        out_shape=jax.ShapeDtypeStruct((regions_total, WIDE), jnp.float32),
        in_specs=[vmem] * 4,
        out_specs=vmem,
        compiler_params=pltpu.CompilerParams(vmem_limit_bytes=VMEM_MIB << 20),
        name="region_table",
    )(region, sample, sums, bin_placement())


def shifted(block, axis, periodic):
    count = lax.axis_size(axis)
    forward = [(i, i + 1) for i in range(count - 1)]
    if periodic:
        forward.append((count - 1, 0))
    backward = [(b, a) for a, b in forward]
    return lax.ppermute(block, axis, forward), lax.ppermute(block, axis, backward)


def on_device(lens_block, lens_count, lens_region, lens_sample, source_block):
    axes = ("ra", "dec")
    bands, band = lax.axis_size("dec"), lax.axis_index("dec")
    regions_total = REG_DEV * lax.axis_size("ra") * bands
    nothing = (((1,), (1,)), ((), ()))

    source = source_block[0, 0]
    source_rank = spatial_order(
        source[ZROWS].astype(jnp.float32), source[ZROWS + 1].astype(jnp.float32), 0.0, 256
    )
    source = lax.dot_general(
        source, order_matrix(source_rank), nothing, preferred_element_type=jnp.float32
    )
    boxes = tile_boxes(source[ZROWS], source[ZROWS + 1])
    boxes = jnp.broadcast_to(boxes.T[:, :, None], (SRC_TILES, 4, LANES)).reshape(SRC_TILES, -1)
    boxes = jnp.pad(boxes, ((BOX_ROW - ZROWS - 5, 0), (0, S_PATCH - 4 * LANES)))
    source = jnp.concatenate([source, boxes], axis=0).astype(jnp.bfloat16)

    low, high = shifted(source, "ra", True)
    middle = jnp.stack([source, low, high])
    columns_at = (0, -1, 1)
    with jax.named_scope("halo_dec"):
        below, above = shifted(middle, "dec", False)

    lens = lens_block[0, 0]
    live = lens_count[0]
    dead = (jnp.arange(L_PATCH, dtype=jnp.int32) >= live[0]).astype(jnp.float32)
    lens_rank = spatial_order(
        lens[ZROWS].astype(jnp.float32), lens[ZROWS + 1].astype(jnp.float32), dead, 64
    )
    order = order_matrix(lens_rank)
    region, sample = lens_region[0], lens_sample[0]
    labels = jnp.concatenate([region // 8, region % 8, sample], axis=0).astype(jnp.bfloat16)
    lens = jnp.concatenate([lens, labels], axis=0)
    columns = lax.dot_general(order, lens, nothing, preferred_element_type=jnp.float32)
    labels = columns[:, ZROWS + 2 :]
    region = (labels[:, 0] * 8.0 + labels[:, 1]).astype(jnp.int32)[None, :]
    sample = labels[:, 2:].astype(jnp.int32)
    place = columns[:, ZROWS : ZROWS + 2]
    wide = jnp.broadcast_to(place.T[:, :, None], (2, L_PATCH, LANES))
    place = place.reshape(LENS_TILES, SUB, 2)
    lens_box = jnp.stack([jnp.min(place, axis=1), jnp.max(place, axis=1)], axis=2)
    lens_box = jnp.pad(lens_box.reshape(LENS_TILES, 4).T, ((0, SUB - 4), (0, LANES - LENS_TILES)))
    where = jnp.stack([band, jnp.int32(bands)]).astype(jnp.int32)

    def pairs(blocks, shifts, before=None, last=False):
        return pair_sums(live, where, columns, wide, lens_box, blocks, shifts, before, last)

    sums = pairs([middle], (tuple((a, 0) for a in columns_at),))
    shifts = tuple(tuple((a, b) for a in columns_at) for b in (-1, 1))
    sums = pairs([below, above], shifts, sums, True)

    table = region_sums(region, sample, sums, regions_total)
    table = lax.all_to_all(table, axes, 0, 0, tiled=True)
    owned = jnp.sum(table.reshape(-1, REG_DEV, WIDE), axis=0)
    owned = owned[:, : 2 * NBIN * SAMPLES].reshape(REG_DEV, SAMPLES, 2, NBIN)
    scales = bin_scales()
    return (owned[:, :, 0, :] / jnp.sqrt(scales), owned[:, :, 1, :] / scales)


def solution(mesh):
    placed = (
        P("ra", "dec", None, None),
        P("ra", "dec"),
        P("ra", "dec", None),
        P("ra", "dec", None),
        P("ra", "dec", None, None),
    )
    return jax.shard_map(
        on_device,
        mesh=mesh,
        in_specs=placed,
        out_specs=(P(("ra", "dec"), None, None), P(("ra", "dec"), None, None)),
        check_vma=False,
    )
```

```python
import functools
import math

import jax
import jax.numpy as jnp
import numpy as np
from jax import lax
from jax.experimental import pallas as pl
from jax.experimental.pallas import tpu as pltpu
from jax.sharding import PartitionSpec as P

NBIN = 20
SAMPLES = 8
PATCH = 256
R_IN = 12
L_PATCH = 512
S_PATCH = 1024
REG_DEV = 8
ZROWS = 128
LANES = 128
SUB = 8
SRC_TILES = S_PATCH // LANES
LENS_TILES = L_PATCH // SUB
UNROLL = (4, 4, 8)
CRIT_ROW = 5 * SUB
FAR = 1.0e6
BOX_ROW = ZROWS + SUB
BLOCK_ROWS = 144
LIST_WORDS = 16
LANE_SUMS = 18
FOLD_SPLIT = 30
VMEM_MIB = 26
THRESHOLD_SUMS = 2 * (NBIN + 1)
WIDE = 3 * LANES
growth_top = 23
growth_bottom = 20


def edge_squares():
    return [
        float((R_IN * growth_top**k // growth_bottom**k) ** 2) for k in range(NBIN + 1)
    ]


EDGES = edge_squares()
GROUPS = ((0, 10), (10, 16), (16, 21))


def bin_scales():
    lens_per_cell = L_PATCH / (SAMPLES * REG_DEV)
    density = S_PATCH / (PATCH * PATCH)
    expected = [
        math.pi * (EDGES[k + 1] - EDGES[k]) * density * lens_per_cell for k in range(NBIN)
    ]
    return jnp.array(expected, jnp.float32)


def tree_sum(terms):
    while len(terms) > 1:
        paired = [a + b for a, b in zip(terms[::2], terms[1::2])]
        terms = paired + ([terms[-1]] if len(terms) % 2 else [])
    return terms[0]


def spatial_order(x, y, dead, group):
    n = x.shape[0]
    index = jnp.arange(n, dtype=jnp.float32)
    key = x * n + index + dead * 2.0**20
    rank = jnp.sum((key[:, None] < key[None, :]).astype(jnp.float32), axis=0)
    key = jnp.floor(rank / group) * 2.0**18 + y * n + index
    return jnp.sum((key[:, None] < key[None, :]).astype(jnp.float32), axis=0)


def order_matrix(rank):
    n = rank.shape[0]
    target = lax.broadcasted_iota(jnp.float32, (n, n), 0)
    return (target == rank[None, :]).astype(jnp.bfloat16)


def tile_boxes(x, y):
    x, y = x.reshape(-1, LANES), y.reshape(-1, LANES)
    return jnp.stack([jnp.min(x, 1), jnp.max(x, 1), jnp.min(y, 1), jnp.max(y, 1)])


def tile_lists(lens_box, boxes, valid, tiles):
    wide = (tiles, LANES)
    gap_x = jnp.maximum(boxes[0] - lens_box[1:2], lens_box[0:1] - boxes[1])
    gap_y = jnp.maximum(boxes[2] - lens_box[3:4], lens_box[2:3] - boxes[3])
    gap_x, gap_y = jnp.maximum(gap_x, 0.0), jnp.maximum(gap_y, 0.0)
    near_sq = jnp.where(valid, gap_x * gap_x + gap_y * gap_y, FAR)
    lower = lax.broadcasted_iota(jnp.int32, (tiles, tiles), 0)
    lower = (lower >= lax.broadcasted_iota(jnp.int32, (tiles, tiles), 1)).astype(jnp.float32)
    lower = lower.astype(jnp.bfloat16)
    tile_id = lax.broadcasted_iota(jnp.int32, wide, 0).astype(jnp.float32) - tiles
    place = jnp.full(wide, -1.0, jnp.float32)
    base = jnp.zeros((1, LANES), jnp.float32)
    inner = jnp.zeros(wide, jnp.float32)
    trips = []
    for group, (_, hi) in enumerate(GROUPS):
        reach = (near_sq < EDGES[hi - 1]).astype(jnp.float32)
        member = (reach - inner).astype(jnp.bfloat16)
        running = jnp.dot(lower, member, preferred_element_type=jnp.float32)
        place = jnp.where(reach > inner, running + (base - 1.0), place)
        inner = reach
        base = base + running[tiles - 1 :]
        trips.append(jnp.floor((base + (UNROLL[group] - 1)) * (1.0 / UNROLL[group])))
    partial = []
    for slot in range(tiles):
        hit = jnp.where(place == float(slot), tile_id, 0.0)
        partial.append(tree_sum([hit[r : r + SUB] for r in range(0, tiles, SUB)]))
    partial = jnp.concatenate(partial, axis=0).astype(jnp.bfloat16)
    words = LIST_WORDS
    row = lax.broadcasted_iota(jnp.int32, (2 * words, tiles * SUB), 0)
    slot = lax.broadcasted_iota(jnp.int32, (2 * words, tiles * SUB), 1) >> 3
    first = 4 * (row & (words - 1)) + 2 * (row >> 4)
    take = jnp.where(slot == first, 1.0, jnp.where(slot == first + 1, 128.0, 0.0))
    packed = jnp.dot(take.astype(jnp.bfloat16), partial, preferred_element_type=jnp.float32)
    packed = (packed + 129.0 * tiles).astype(jnp.int32)
    packed = packed[:words] + packed[words:] * (1 << 14)
    row = lax.broadcasted_iota(jnp.int32, (SUB, LANES), 0)
    counts = jnp.where(row == 0, trips[0], jnp.where(row == 1, trips[1], trips[2]))
    return jnp.concatenate([packed, counts.astype(jnp.int32)], axis=0)


def pair_kernel(shifts, later, last, *refs):
    n = sum(len(group) for group in shifts)
    tiles = n * SRC_TILES
    live_ref, band_ref, columns_ref, place_ref, box_ref = refs[:5]
    blocks = refs[5 : 5 + len(shifts)]
    rest = refs[5 + len(shifts) :]
    before_ref = None
    if later:
        before_ref, *rest = rest
    if last:
        fold_ref, out_ref, *rest = rest
    sums, *rest = rest
    tables, slots, list_vmem, list_ref, list_sem = rest
    live = live_ref[0]
    tile_shape = (SUB, LANES)
    patches = [
        (block, at, shift)
        for block, group in zip(blocks, shifts)
        for at, shift in enumerate(group)
    ]

    boxes, valid = [[] for _ in range(4)], []
    for block, at, shift in patches:
        for c in range(4):
            part = block[at, BOX_ROW : BOX_ROW + SUB, c * LANES : (c + 1) * LANES]
            boxes[c].append(part.astype(jnp.float32) + shift[c // 2] * PATCH)
        there = band_ref[0] + shift[1]
        inside = (there >= 0) & (there < band_ref[1])
        valid.append(jnp.full(tile_shape, inside.astype(jnp.float32)))
    boxes = [jnp.concatenate(box, axis=0) for box in boxes]
    valid = jnp.concatenate(valid, axis=0) > 0.0
    list_vmem[...] = tile_lists(box_ref[...], boxes, valid, tiles)
    copy = pltpu.make_async_copy(list_vmem, list_ref, list_sem)
    copy.start()

    for p, (block, at, (shift_x, shift_y)) in enumerate(patches):
        rows = block[at, ZROWS : ZROWS + 5, :].astype(jnp.float32)
        weight = rows[4:5]
        values = (
            rows[0:1] + shift_x * PATCH,
            rows[1:2] + shift_y * PATCH,
            -(weight * rows[2:3]),
            -2.0 * (weight * rows[3:4]),
            weight,
        )
        for t in range(SRC_TILES):
            for v, value in enumerate(values):
                tables[p * SRC_TILES + t, v * SUB : (v + 1) * SUB] = jnp.broadcast_to(
                    value[:, t * LANES : (t + 1) * LANES], tile_shape
                )
    for v in range(5):
        tables[tiles, v * SUB : (v + 1) * SUB] = jnp.full(
            tile_shape, FAR if v == 0 else 0.0, jnp.float32
        )
    tables[tiles, CRIT_ROW:] = jnp.zeros((L_PATCH, LANES), jnp.float32)

    def crit_step(chunk, carry):
        first = pl.multiple_of(chunk * LANES, LANES)
        kernel_rows = columns_ref[pl.ds(first, LANES), :ZROWS].astype(jnp.bfloat16)
        for p, (block, at, _) in enumerate(patches):
            product = jnp.dot(
                kernel_rows, block[at, :ZROWS, :], preferred_element_type=jnp.float32
            )
            for t in range(SRC_TILES):
                tables[p * SRC_TILES + t, pl.ds(CRIT_ROW + first, LANES), :] = product[
                    :, t * LANES : (t + 1) * LANES
                ]
        return carry

    lax.fori_loop(0, (live + LANES - 1) // LANES, crit_step, 0)
    copy.wait()

    def add_up(rows, terms, group):
        for k in range(*GROUPS[group]):
            inside = [r2 < EDGES[k] for _, _, r2 in terms]
            for c in range(2):
                picked = [jnp.where(m, t[c], 0.0) for m, t in zip(inside, terms)]
                at = c * (NBIN + 1) + k
                sums[at, rows, :] = sums[at, rows, :] + tree_sum(picked)

    def lens_step(lens_tile, base):
        first = pl.multiple_of(lens_tile * SUB, SUB)
        rows = pl.ds(pl.multiple_of(first - base, SUB), SUB)
        trips = [list_ref[LIST_WORDS + group, lens_tile] for group in range(3)]
        lens_x = place_ref[0, pl.ds(first, SUB), :]
        lens_y = place_ref[1, pl.ds(first, SUB), :]
        for v in range(THRESHOLD_SUMS):
            sums[v, rows, :] = (
                before_ref[v, pl.ds(first, SUB), :] if later else jnp.zeros(tile_shape, jnp.float32)
            )

        def far_step(i, words):
            following = (list_ref[2 * i + 2, lens_tile], list_ref[2 * i + 3, lens_tile])
            terms = []
            for u in range(UNROLL[2]):
                tile = (words[u // 4] >> (7 * (u % 4))) & 127
                dx, dy = tables[tile, 0:SUB] - lens_x, tables[tile, SUB : 2 * SUB] - lens_y
                dx_sq, dy_sq = dx * dx, dy * dy
                r2 = dx_sq + dy_sq
                turned = tables[tile, 2 * SUB : 3 * SUB] * (dx_sq - dy_sq)
                turned = turned + tables[tile, 3 * SUB : 4 * SUB] * (dx * dy)
                value = tables[tile, pl.ds(CRIT_ROW + first, SUB), :]
                signal = value * (turned / jnp.maximum(r2, EDGES[0]))
                weight = tables[tile, 4 * SUB : 5 * SUB] * value * value
                slots[0, i * UNROLL[2] + u] = signal
                slots[1, i * UNROLL[2] + u] = weight
                slots[2, i * UNROLL[2] + u] = r2
                terms.append((signal, weight, r2))
            add_up(rows, terms, 2)
            return following

        lax.fori_loop(0, trips[2], far_step, (list_ref[0, lens_tile], list_ref[1, lens_tile]))
        for group in (1, 0):

            def near_step(i, nothing, group=group):
                terms = [
                    tuple(slots[c, i * UNROLL[group] + u] for c in range(3))
                    for u in range(UNROLL[group])
                ]
                add_up(rows, terms, group)
                return nothing

            lax.fori_loop(0, trips[group], near_step, 0)
        return base

    lens_tiles = live // SUB
    if not last:
        lax.fori_loop(0, lens_tiles, lens_step, 0)
        return
    out_ref[...] = jnp.zeros_like(out_ref)

    def chunk_step(chunk, carry):
        first = pl.multiple_of(chunk * LANES, LANES)
        tiles_first = chunk * (LANES // SUB)
        tiles_end = jnp.minimum(tiles_first + LANES // SUB, lens_tiles)
        lax.fori_loop(tiles_first, tiles_end, lens_step, first)
        high, low = [], []
        for v in range(LANE_SUMS, THRESHOLD_SUMS):
            value = sums[v]
            high.append(value.astype(jnp.bfloat16))
            low.append((value - high[-1].astype(jnp.float32)).astype(jnp.bfloat16))
        folded = []
        for lo, hi in ((LANE_SUMS, FOLD_SPLIT), (FOLD_SPLIT, THRESHOLD_SUMS)):
            both = [
                jnp.concatenate(part[lo - LANE_SUMS : hi - LANE_SUMS], axis=1)
                for part in (high, low)
            ]
            weights = fold_ref[lo * LANES : hi * LANES, :]
            folded += [jnp.dot(p, weights, preferred_element_type=jnp.float32) for p in both]
        folded = tree_sum(folded)
        lane = lax.broadcasted_iota(jnp.int32, (LANES, LANES), 1)
        for v in range(LANE_SUMS):
            folded = jnp.where(lane == v, jnp.sum(sums[v], axis=1, keepdims=True), folded)
        row = lax.broadcasted_iota(jnp.int32, (LANES, LANES), 0) + first
        folded = jnp.where(row < live, folded, 0.0)
        out_ref[pl.ds(first, LANES), :] = folded
        return carry

    lax.fori_loop(0, (live + LANES - 1) // LANES, chunk_step, 0)


def fold_matrix():
    matrix = np.zeros((THRESHOLD_SUMS, LANES, LANES), np.float32)
    for v in range(THRESHOLD_SUMS):
        matrix[v, :, v] = 1.0
    return jnp.asarray(matrix.reshape(-1, LANES), jnp.bfloat16)


def pair_sums(live, bands, columns, place, lens_box, blocks, shifts, before=None, last=False):
    n = sum(len(group) for group in shifts)
    tiles = n * SRC_TILES
    later = before is not None
    smem = pl.BlockSpec(memory_space=pltpu.SMEM)
    vmem = pl.BlockSpec(memory_space=pltpu.VMEM)
    all_sums = (THRESHOLD_SUMS, L_PATCH, LANES)
    scratch = [
        pltpu.VMEM((tiles + 1, CRIT_ROW + L_PATCH, LANES), jnp.float32),
        pltpu.VMEM((3, tiles, SUB, LANES), jnp.float32),
        pltpu.VMEM((LIST_WORDS + SUB, LANES), jnp.int32),
        pltpu.SMEM((LIST_WORDS + SUB, LANES), jnp.int32),
        pltpu.SemaphoreType.DMA,
    ]
    operands = (live, bands, columns, place, lens_box, *blocks)
    operands += (before,) if later else ()
    operands += (fold_matrix(),) if last else ()
    return pl.pallas_call(
        functools.partial(pair_kernel, shifts, later, last),
        out_shape=jax.ShapeDtypeStruct((L_PATCH, LANES) if last else all_sums, jnp.float32),
        in_specs=[smem] * 2 + [vmem] * (len(operands) - 2),
        out_specs=vmem,
        input_output_aliases={5 + len(blocks): 0} if later and not last else {},
        scratch_shapes=([pltpu.VMEM((THRESHOLD_SUMS, LANES, LANES), jnp.float32)] if last else []) + scratch,
        cost_estimate=pl.CostEstimate(
            flops=n * 20_000_000_000, transcendentals=0, bytes_accessed=n * 300_000
        ),
        compiler_params=pltpu.CompilerParams(vmem_limit_bytes=VMEM_MIB << 20),
        name=f"pairs_{n}",
    )(*operands)


def split_parts(value):
    parts = []
    for _ in range(3):
        part = value.astype(jnp.bfloat16)
        value = value - part.astype(jnp.float32)
        parts.append(part)
    return parts


def bin_placement():
    matrix = np.zeros((LANES, WIDE), np.float32)
    for m in range(SAMPLES):
        for c in range(2):
            for k in range(NBIN):
                column = (m * 2 + c) * NBIN + k
                matrix[c * (NBIN + 1) + k + 1, column] = 1.0
                matrix[c * (NBIN + 1) + k, column] = -1.0
    return jnp.asarray(matrix, jnp.bfloat16)


def table_kernel(region_ref, sample_ref, sums_ref, place_ref, out_ref):
    def product(matrices, others):
        return tree_sum(
            [jnp.dot(a, b, preferred_element_type=jnp.float32) for a, b in zip(matrices, others)][::-1]
        )

    bins = product(split_parts(sums_ref[...]), [place_ref[...]] * 3)
    lane = lax.broadcasted_iota(jnp.int32, bins.shape, 1) - sample_ref[...] * (2 * NBIN)
    bins = jnp.where((lane >= 0) & (lane < 2 * NBIN), bins, 0.0)
    region = region_ref[...]
    ids = lax.broadcasted_iota(jnp.int32, (out_ref.shape[0], region.shape[1]), 0)
    match = (ids == region).astype(jnp.float32).astype(jnp.bfloat16)
    out_ref[...] = product([match] * 2, split_parts(bins)[:2])


def region_sums(region, sample, sums, regions_total):
    vmem = pl.BlockSpec(memory_space=pltpu.VMEM)
    return pl.pallas_call(
        table_kernel,
        out_shape=jax.ShapeDtypeStruct((regions_total, WIDE), jnp.float32),
        in_specs=[vmem] * 4,
        out_specs=vmem,
        compiler_params=pltpu.CompilerParams(vmem_limit_bytes=VMEM_MIB << 20),
        name="region_table",
    )(region, sample, sums, bin_placement())


def shifted(block, axis, periodic):
    count = lax.axis_size(axis)
    forward = [(i, i + 1) for i in range(count - 1)]
    if periodic:
        forward.append((count - 1, 0))
    backward = [(b, a) for a, b in forward]
    return lax.ppermute(block, axis, forward), lax.ppermute(block, axis, backward)


def on_device(lens_block, lens_count, lens_region, lens_sample, source_block):
    axes = ("ra", "dec")
    bands, band = lax.axis_size("dec"), lax.axis_index("dec")
    regions_total = REG_DEV * lax.axis_size("ra") * bands
    nothing = (((1,), (1,)), ((), ()))

    source = source_block[0, 0]
    source_rank = spatial_order(
        source[ZROWS].astype(jnp.float32), source[ZROWS + 1].astype(jnp.float32), 0.0, 256
    )
    source = lax.dot_general(
        source, order_matrix(source_rank), nothing, preferred_element_type=jnp.float32
    )
    boxes = tile_boxes(source[ZROWS], source[ZROWS + 1])
    boxes = jnp.broadcast_to(boxes.T[:, :, None], (SRC_TILES, 4, LANES)).reshape(SRC_TILES, -1)
    boxes = jnp.pad(boxes, ((BOX_ROW - ZROWS - 5, 0), (0, S_PATCH - 4 * LANES)))
    source = jnp.concatenate([source, boxes], axis=0).astype(jnp.bfloat16)

    low, high = shifted(source, "ra", True)
    middle = jnp.stack([source, low, high])
    columns_at = (0, -1, 1)
    with jax.named_scope("halo_dec"):
        below, above = shifted(middle, "dec", False)

    lens = lens_block[0, 0]
    live = lens_count[0]
    dead = (jnp.arange(L_PATCH, dtype=jnp.int32) >= live[0]).astype(jnp.float32)
    lens_rank = spatial_order(
        lens[ZROWS].astype(jnp.float32), lens[ZROWS + 1].astype(jnp.float32), dead, 64
    )
    order = order_matrix(lens_rank)
    region, sample = lens_region[0], lens_sample[0]
    labels = jnp.concatenate([region // 8, region % 8, sample], axis=0).astype(jnp.bfloat16)
    lens = jnp.concatenate([lens, labels], axis=0)
    columns = lax.dot_general(order, lens, nothing, preferred_element_type=jnp.float32)
    labels = columns[:, ZROWS + 2 :]
    region = (labels[:, 0] * 8.0 + labels[:, 1]).astype(jnp.int32)[None, :]
    sample = labels[:, 2:].astype(jnp.int32)
    place = columns[:, ZROWS : ZROWS + 2]
    wide = jnp.broadcast_to(place.T[:, :, None], (2, L_PATCH, LANES))
    place = place.reshape(LENS_TILES, SUB, 2)
    lens_box = jnp.stack([jnp.min(place, axis=1), jnp.max(place, axis=1)], axis=2)
    lens_box = jnp.pad(lens_box.reshape(LENS_TILES, 4).T, ((0, SUB - 4), (0, LANES - LENS_TILES)))
    where = jnp.stack([band, jnp.int32(bands)]).astype(jnp.int32)

    def pairs(blocks, shifts, before=None, last=False):
        return pair_sums(live, where, columns, wide, lens_box, blocks, shifts, before, last)

    sums = pairs([middle], (tuple((a, 0) for a in columns_at),))
    shifts = tuple(tuple((a, b) for a in columns_at) for b in (-1, 1))
    sums = pairs([below, above], shifts, sums, True)

    table = region_sums(region, sample, sums, regions_total)
    table = lax.all_to_all(table, axes, 0, 0, tiled=True)
    owned = jnp.sum(table.reshape(-1, REG_DEV, WIDE), axis=0)
    owned = owned[:, : 2 * NBIN * SAMPLES].reshape(REG_DEV, SAMPLES, 2, NBIN)
    scales = bin_scales()
    return (owned[:, :, 0, :] / jnp.sqrt(scales), owned[:, :, 1, :] / scales)


def solution(mesh):
    placed = (
        P("ra", "dec", None, None),
        P("ra", "dec"),
        P("ra", "dec", None),
        P("ra", "dec", None),
        P("ra", "dec", None, None),
    )
    return jax.shard_map(
        on_device,
        mesh=mesh,
        in_specs=placed,
        out_specs=(P(("ra", "dec"), None, None), P(("ra", "dec"), None, None)),
        check_vma=False,
    )
```

```python
import functools
import math

import jax
import jax.numpy as jnp
import numpy as np
from jax import lax
from jax.experimental import pallas as pl
from jax.experimental.pallas import tpu as pltpu
from jax.sharding import PartitionSpec as P

NBIN = 20
SAMPLES = 8
PATCH = 256
R_IN = 12
L_PATCH = 512
S_PATCH = 1024
REG_DEV = 8
ZROWS = 128
LANES = 128
SUB = 8
SRC_TILES = S_PATCH // LANES
LENS_TILES = L_PATCH // SUB
UNROLL = (4, 4, 8)
CRIT_ROW = 5 * SUB
FAR = 1.0e6
BOX_ROW = ZROWS + SUB
BLOCK_ROWS = 144
LIST_WORDS = 16
LANE_SUMS = 18
FOLD_SPLIT = 30
VMEM_MIB = 26
THRESHOLD_SUMS = 2 * (NBIN + 1)
WIDE = 3 * LANES
growth_top = 23
growth_bottom = 20


def edge_squares():
    return [
        float((R_IN * growth_top**k // growth_bottom**k) ** 2) for k in range(NBIN + 1)
    ]


EDGES = edge_squares()
GROUPS = ((0, 10), (10, 16), (16, 21))


def lane_scales():
    lens_per_cell = L_PATCH / (SAMPLES * REG_DEV)
    density = S_PATCH / (PATCH * PATCH)
    expected = [
        math.pi * (EDGES[k + 1] - EDGES[k]) * density * lens_per_cell for k in range(NBIN)
    ]
    expected = np.array(expected, np.float32)
    row = np.ones((1, WIDE), np.float32)
    row[0, : 2 * NBIN * SAMPLES] = np.tile(np.stack([np.sqrt(expected), expected]).ravel(), SAMPLES)
    return jnp.asarray(row)


def tree_sum(terms):
    while len(terms) > 1:
        paired = [a + b for a, b in zip(terms[::2], terms[1::2])]
        terms = paired + ([terms[-1]] if len(terms) % 2 else [])
    return terms[0]


def spatial_order(x, y, dead, group):
    n = x.shape[0]
    index = jnp.arange(n, dtype=jnp.float32)
    key = x * n + index + dead * 2.0**20
    rank = jnp.sum((key[:, None] < key[None, :]).astype(jnp.float32), axis=0)
    key = jnp.floor(rank / group) * 2.0**18 + y * n + index
    return jnp.sum((key[:, None] < key[None, :]).astype(jnp.float32), axis=0)


def order_matrix(rank):
    n = rank.shape[0]
    target = lax.broadcasted_iota(jnp.float32, (n, n), 0)
    return (target == rank[None, :]).astype(jnp.bfloat16)


def column_of(row):
    return jnp.transpose(jnp.broadcast_to(row, (LANES, row.shape[1])))


def row_ranks(row):
    column = column_of(row)
    ranks = []
    for first in range(0, row.shape[1], LANES):
        below = jnp.where(column < row[:, first : first + LANES], 1.0, 0.0)
        ranks.append(jnp.sum(below, axis=0, keepdims=True))
    return jnp.concatenate(ranks, axis=1)


def source_kernel(source_ref, out_ref):
    n = S_PATCH
    index = lax.broadcasted_iota(jnp.int32, (1, n), 1).astype(jnp.float32)
    place = source_ref[ZROWS : ZROWS + 2, :].astype(jnp.float32)
    rank = row_ranks(place[0:1] * n + index)
    key = jnp.floor(rank * (1.0 / 256)) * 2.0**18 + place[1:2] * n + index
    rank = column_of(row_ranks(key))
    lane = lax.broadcasted_iota(jnp.int32, (n, LANES), 1).astype(jnp.float32)
    row = lax.broadcasted_iota(jnp.int32, (SRC_TILES, LANES), 0)
    boxes = [jnp.zeros((SRC_TILES, LANES), jnp.float32) for _ in range(4)]
    for first in range(0, n, 2 * LANES):
        match = jnp.concatenate(
            [jnp.where(rank == lane + float(first + at), 1.0, 0.0) for at in (0, LANES)], axis=1
        )
        ordered = jnp.dot(
            source_ref[...], match.astype(jnp.bfloat16), preferred_element_type=jnp.float32
        )
        out_ref[: ZROWS + 5, first : first + 2 * LANES] = ordered.astype(jnp.bfloat16)
        for at in (0, LANES):
            for c in range(4):
                values = ordered[ZROWS + c // 2 : ZROWS + c // 2 + 1, at : at + LANES]
                reduce = jnp.max if c % 2 else jnp.min
                bound = reduce(values, axis=1, keepdims=True)
                boxes[c] = jnp.where(row == (first + at) // LANES, bound, boxes[c])
    boxes = jnp.concatenate(boxes, axis=1).astype(jnp.bfloat16)
    out_ref[BOX_ROW:, : 4 * LANES] = boxes


def ordered_sources(source):
    vmem = pl.BlockSpec(memory_space=pltpu.VMEM)
    return pl.pallas_call(
        source_kernel,
        out_shape=jax.ShapeDtypeStruct((BLOCK_ROWS, S_PATCH), jnp.bfloat16),
        in_specs=[vmem],
        out_specs=vmem,
        compiler_params=pltpu.CompilerParams(vmem_limit_bytes=VMEM_MIB << 20),
        name="order_sources",
    )(source)


def tile_lists(lens_box, boxes, valid, tiles):
    wide = (tiles, LANES)
    gap_x = jnp.maximum(boxes[0] - lens_box[1:2], lens_box[0:1] - boxes[1])
    gap_y = jnp.maximum(boxes[2] - lens_box[3:4], lens_box[2:3] - boxes[3])
    gap_x, gap_y = jnp.maximum(gap_x, 0.0), jnp.maximum(gap_y, 0.0)
    near_sq = jnp.where(valid, gap_x * gap_x + gap_y * gap_y, FAR)
    lower = lax.broadcasted_iota(jnp.int32, (tiles, tiles), 0)
    lower = (lower >= lax.broadcasted_iota(jnp.int32, (tiles, tiles), 1)).astype(jnp.float32)
    lower = lower.astype(jnp.bfloat16)
    tile_id = lax.broadcasted_iota(jnp.int32, wide, 0).astype(jnp.float32) - tiles
    place = jnp.full(wide, -1.0, jnp.float32)
    base = jnp.zeros((1, LANES), jnp.float32)
    inner = jnp.zeros(wide, jnp.float32)
    trips = []
    for group, (_, hi) in enumerate(GROUPS):
        reach = (near_sq < EDGES[hi - 1]).astype(jnp.float32)
        member = (reach - inner).astype(jnp.bfloat16)
        running = jnp.dot(lower, member, preferred_element_type=jnp.float32)
        place = jnp.where(reach > inner, running + (base - 1.0), place)
        inner = reach
        base = base + running[tiles - 1 :]
        trips.append(jnp.floor((base + (UNROLL[group] - 1)) * (1.0 / UNROLL[group])))
    partial = []
    for slot in range(tiles):
        hit = jnp.where(place == float(slot), tile_id, 0.0)
        partial.append(tree_sum([hit[r : r + SUB] for r in range(0, tiles, SUB)]))
    partial = jnp.concatenate(partial, axis=0).astype(jnp.bfloat16)
    words = LIST_WORDS
    row = lax.broadcasted_iota(jnp.int32, (2 * words, tiles * SUB), 0)
    slot = lax.broadcasted_iota(jnp.int32, (2 * words, tiles * SUB), 1) >> 3
    first = 4 * (row & (words - 1)) + 2 * (row >> 4)
    take = jnp.where(slot == first, 1.0, jnp.where(slot == first + 1, 128.0, 0.0))
    packed = jnp.dot(take.astype(jnp.bfloat16), partial, preferred_element_type=jnp.float32)
    packed = (packed + 129.0 * tiles).astype(jnp.int32)
    packed = packed[:words] + packed[words:] * (1 << 14)
    row = lax.broadcasted_iota(jnp.int32, (SUB, LANES), 0)
    counts = jnp.where(row == 0, trips[0], jnp.where(row == 1, trips[1], trips[2]))
    return jnp.concatenate([packed, counts.astype(jnp.int32)], axis=0)


def pair_kernel(shifts, later, last, *refs):
    n = sum(len(group) for group in shifts)
    tiles = n * SRC_TILES
    live_ref, band_ref, columns_ref, place_ref, box_ref = refs[:5]
    blocks = refs[5 : 5 + len(shifts)]
    rest = refs[5 + len(shifts) :]
    before_ref = None
    if later:
        before_ref, *rest = rest
    if last:
        fold_ref, out_ref, *rest = rest
    sums, *rest = rest
    tables, slots, list_vmem, list_ref, list_sem = rest
    live = live_ref[0]
    tile_shape = (SUB, LANES)
    patches = [
        (block, at, shift)
        for block, group in zip(blocks, shifts)
        for at, shift in enumerate(group)
    ]

    boxes, valid = [[] for _ in range(4)], []
    for block, at, shift in patches:
        for c in range(4):
            part = block[at, BOX_ROW : BOX_ROW + SUB, c * LANES : (c + 1) * LANES]
            boxes[c].append(part.astype(jnp.float32) + shift[c // 2] * PATCH)
        there = band_ref[0] + shift[1]
        inside = (there >= 0) & (there < band_ref[1])
        valid.append(jnp.full(tile_shape, inside.astype(jnp.float32)))
    boxes = [jnp.concatenate(box, axis=0) for box in boxes]
    valid = jnp.concatenate(valid, axis=0) > 0.0
    list_vmem[...] = tile_lists(box_ref[...], boxes, valid, tiles)
    copy = pltpu.make_async_copy(list_vmem, list_ref, list_sem)
    copy.start()

    for p, (block, at, (shift_x, shift_y)) in enumerate(patches):
        rows = block[at, ZROWS : ZROWS + 5, :].astype(jnp.float32)
        weight = rows[4:5]
        values = (
            rows[0:1] + shift_x * PATCH,
            rows[1:2] + shift_y * PATCH,
            -(weight * rows[2:3]),
            -2.0 * (weight * rows[3:4]),
            weight,
        )
        for t in range(SRC_TILES):
            for v, value in enumerate(values):
                tables[p * SRC_TILES + t, v * SUB : (v + 1) * SUB] = jnp.broadcast_to(
                    value[:, t * LANES : (t + 1) * LANES], tile_shape
                )
    for v in range(5):
        tables[tiles, v * SUB : (v + 1) * SUB] = jnp.full(
            tile_shape, FAR if v == 0 else 0.0, jnp.float32
        )
    tables[tiles, CRIT_ROW:] = jnp.zeros((L_PATCH, LANES), jnp.float32)

    def crit_step(chunk, carry):
        first = pl.multiple_of(chunk * LANES, LANES)
        kernel_rows = columns_ref[pl.ds(first, LANES), :ZROWS].astype(jnp.bfloat16)
        for p, (block, at, _) in enumerate(patches):
            product = jnp.dot(
                kernel_rows, block[at, :ZROWS, :], preferred_element_type=jnp.float32
            )
            for t in range(SRC_TILES):
                tables[p * SRC_TILES + t, pl.ds(CRIT_ROW + first, LANES), :] = product[
                    :, t * LANES : (t + 1) * LANES
                ]
        return carry

    lax.fori_loop(0, (live + LANES - 1) // LANES, crit_step, 0)
    copy.wait()

    def add_up(rows, terms, group):
        for k in range(*GROUPS[group]):
            inside = [r2 < EDGES[k] for _, _, r2 in terms]
            for c in range(2):
                picked = [jnp.where(m, t[c], 0.0) for m, t in zip(inside, terms)]
                at = c * (NBIN + 1) + k
                sums[at, rows, :] = sums[at, rows, :] + tree_sum(picked)

    def lens_step(lens_tile, base):
        first = pl.multiple_of(lens_tile * SUB, SUB)
        rows = pl.ds(pl.multiple_of(first - base, SUB), SUB)
        trips = [list_ref[LIST_WORDS + group, lens_tile] for group in range(3)]
        lens_x = place_ref[0, pl.ds(first, SUB), :]
        lens_y = place_ref[1, pl.ds(first, SUB), :]
        for v in range(THRESHOLD_SUMS):
            sums[v, rows, :] = (
                before_ref[v, pl.ds(first, SUB), :] if later else jnp.zeros(tile_shape, jnp.float32)
            )

        def far_step(i, words):
            following = (list_ref[2 * i + 2, lens_tile], list_ref[2 * i + 3, lens_tile])
            terms = []
            for u in range(UNROLL[2]):
                tile = (words[u // 4] >> (7 * (u % 4))) & 127
                dx, dy = tables[tile, 0:SUB] - lens_x, tables[tile, SUB : 2 * SUB] - lens_y
                dx_sq, dy_sq = dx * dx, dy * dy
                r2 = dx_sq + dy_sq
                turned = tables[tile, 2 * SUB : 3 * SUB] * (dx_sq - dy_sq)
                turned = turned + tables[tile, 3 * SUB : 4 * SUB] * (dx * dy)
                value = tables[tile, pl.ds(CRIT_ROW + first, SUB), :]
                signal = value * (turned / jnp.maximum(r2, EDGES[0]))
                weight = tables[tile, 4 * SUB : 5 * SUB] * value * value
                slots[0, i * UNROLL[2] + u] = signal
                slots[1, i * UNROLL[2] + u] = weight
                slots[2, i * UNROLL[2] + u] = r2
                terms.append((signal, weight, r2))
            add_up(rows, terms, 2)
            return following

        lax.fori_loop(0, trips[2], far_step, (list_ref[0, lens_tile], list_ref[1, lens_tile]))
        for group in (1, 0):

            def near_step(i, nothing, group=group):
                terms = [
                    tuple(slots[c, i * UNROLL[group] + u] for c in range(3))
                    for u in range(UNROLL[group])
                ]
                add_up(rows, terms, group)
                return nothing

            lax.fori_loop(0, trips[group], near_step, 0)
        return base

    lens_tiles = live // SUB
    if not last:
        lax.fori_loop(0, lens_tiles, lens_step, 0)
        return
    out_ref[...] = jnp.zeros_like(out_ref)

    def chunk_step(chunk, carry):
        first = pl.multiple_of(chunk * LANES, LANES)
        tiles_first = chunk * (LANES // SUB)
        tiles_end = jnp.minimum(tiles_first + LANES // SUB, lens_tiles)
        lax.fori_loop(tiles_first, tiles_end, lens_step, first)
        high, low = [], []
        for v in range(LANE_SUMS, THRESHOLD_SUMS):
            value = sums[v]
            high.append(value.astype(jnp.bfloat16))
            low.append((value - high[-1].astype(jnp.float32)).astype(jnp.bfloat16))
        folded = []
        for lo, hi in ((LANE_SUMS, FOLD_SPLIT), (FOLD_SPLIT, THRESHOLD_SUMS)):
            both = [
                jnp.concatenate(part[lo - LANE_SUMS : hi - LANE_SUMS], axis=1)
                for part in (high, low)
            ]
            weights = fold_ref[lo * LANES : hi * LANES, :]
            folded += [jnp.dot(p, weights, preferred_element_type=jnp.float32) for p in both]
        folded = tree_sum(folded)
        lane = lax.broadcasted_iota(jnp.int32, (LANES, LANES), 1)
        for v in range(LANE_SUMS):
            folded = jnp.where(lane == v, jnp.sum(sums[v], axis=1, keepdims=True), folded)
        row = lax.broadcasted_iota(jnp.int32, (LANES, LANES), 0) + first
        folded = jnp.where(row < live, folded, 0.0)
        out_ref[pl.ds(first, LANES), :] = folded
        return carry

    lax.fori_loop(0, (live + LANES - 1) // LANES, chunk_step, 0)


def fold_matrix():
    matrix = np.zeros((THRESHOLD_SUMS, LANES, LANES), np.float32)
    for v in range(THRESHOLD_SUMS):
        matrix[v, :, v] = 1.0
    return jnp.asarray(matrix.reshape(-1, LANES), jnp.bfloat16)


def pair_sums(live, bands, columns, place, lens_box, blocks, shifts, before=None, last=False):
    n = sum(len(group) for group in shifts)
    tiles = n * SRC_TILES
    later = before is not None
    smem = pl.BlockSpec(memory_space=pltpu.SMEM)
    vmem = pl.BlockSpec(memory_space=pltpu.VMEM)
    all_sums = (THRESHOLD_SUMS, L_PATCH, LANES)
    scratch = [
        pltpu.VMEM((tiles + 1, CRIT_ROW + L_PATCH, LANES), jnp.float32),
        pltpu.VMEM((3, tiles, SUB, LANES), jnp.float32),
        pltpu.VMEM((LIST_WORDS + SUB, LANES), jnp.int32),
        pltpu.SMEM((LIST_WORDS + SUB, LANES), jnp.int32),
        pltpu.SemaphoreType.DMA,
    ]
    operands = (live, bands, columns, place, lens_box, *blocks)
    operands += (before,) if later else ()
    operands += (fold_matrix(),) if last else ()
    return pl.pallas_call(
        functools.partial(pair_kernel, shifts, later, last),
        out_shape=jax.ShapeDtypeStruct((L_PATCH, LANES) if last else all_sums, jnp.float32),
        in_specs=[smem] * 2 + [vmem] * (len(operands) - 2),
        out_specs=vmem,
        input_output_aliases={5 + len(blocks): 0} if later and not last else {},
        scratch_shapes=([pltpu.VMEM((THRESHOLD_SUMS, LANES, LANES), jnp.float32)] if last else []) + scratch,
        cost_estimate=pl.CostEstimate(
            flops=n * 20_000_000_000, transcendentals=0, bytes_accessed=n * 300_000
        ),
        compiler_params=pltpu.CompilerParams(vmem_limit_bytes=VMEM_MIB << 20),
        name=f"pairs_{n}",
    )(*operands)


def split_parts(value):
    parts = []
    for _ in range(3):
        part = value.astype(jnp.bfloat16)
        value = value - part.astype(jnp.float32)
        parts.append(part)
    return parts


def bin_placement():
    matrix = np.zeros((LANES, WIDE), np.float32)
    for m in range(SAMPLES):
        for c in range(2):
            for k in range(NBIN):
                column = (m * 2 + c) * NBIN + k
                matrix[c * (NBIN + 1) + k + 1, column] = 1.0
                matrix[c * (NBIN + 1) + k, column] = -1.0
    return jnp.asarray(matrix, jnp.bfloat16)


def table_kernel(region_ref, sample_ref, sums_ref, place_ref, out_ref):
    def product(matrices, others):
        return tree_sum(
            [jnp.dot(a, b, preferred_element_type=jnp.float32) for a, b in zip(matrices, others)][::-1]
        )

    bins = product(split_parts(sums_ref[...]), [place_ref[...]] * 3)
    lane = lax.broadcasted_iota(jnp.int32, bins.shape, 1) - sample_ref[...] * (2 * NBIN)
    bins = jnp.where((lane >= 0) & (lane < 2 * NBIN), bins, 0.0)
    region = region_ref[...]
    ids = lax.broadcasted_iota(jnp.int32, (out_ref.shape[0], region.shape[1]), 0)
    match = (ids == region).astype(jnp.float32).astype(jnp.bfloat16)
    out_ref[...] = product([match] * 2, split_parts(bins)[:2])


def region_sums(region, sample, sums, regions_total):
    vmem = pl.BlockSpec(memory_space=pltpu.VMEM)
    return pl.pallas_call(
        table_kernel,
        out_shape=jax.ShapeDtypeStruct((regions_total, WIDE), jnp.float32),
        in_specs=[vmem] * 4,
        out_specs=vmem,
        compiler_params=pltpu.CompilerParams(vmem_limit_bytes=VMEM_MIB << 20),
        name="region_table",
    )(region, sample, sums, bin_placement())


def owned_kernel(parts_ref, scale_ref, signal_ref, weight_ref):
    total = jnp.sum(parts_ref[...], axis=0) / scale_ref[...]
    for m in range(SAMPLES):
        for c, out_ref in enumerate((signal_ref, weight_ref)):
            first = (2 * m + c) * NBIN
            out_ref[:, m, :] = total[:, first : first + NBIN]


def owned_sums(parts):
    vmem = pl.BlockSpec(memory_space=pltpu.VMEM)
    out = jax.ShapeDtypeStruct((REG_DEV, SAMPLES, NBIN), jnp.float32)
    return pl.pallas_call(
        owned_kernel,
        out_shape=(out, out),
        in_specs=[vmem] * 2,
        out_specs=(vmem, vmem),
        compiler_params=pltpu.CompilerParams(vmem_limit_bytes=VMEM_MIB << 20),
        name="owned_sums",
    )(parts, lane_scales())


def shifted(block, axis, periodic):
    count = lax.axis_size(axis)
    forward = [(i, i + 1) for i in range(count - 1)]
    if periodic:
        forward.append((count - 1, 0))
    backward = [(b, a) for a, b in forward]
    return lax.ppermute(block, axis, forward), lax.ppermute(block, axis, backward)


def on_device(lens_block, lens_count, lens_region, lens_sample, source_block):
    axes = ("ra", "dec")
    bands, band = lax.axis_size("dec"), lax.axis_index("dec")
    regions_total = REG_DEV * lax.axis_size("ra") * bands
    nothing = (((1,), (1,)), ((), ()))

    source = ordered_sources(source_block[0, 0])
    low, high = shifted(source, "ra", True)
    middle = jnp.stack([source, low, high])
    columns_at = (0, -1, 1)
    with jax.named_scope("halo_dec"):
        below, above = shifted(middle, "dec", False)

    lens = lens_block[0, 0]
    live = lens_count[0]
    dead = (jnp.arange(L_PATCH, dtype=jnp.int32) >= live[0]).astype(jnp.float32)
    lens_rank = spatial_order(
        lens[ZROWS].astype(jnp.float32), lens[ZROWS + 1].astype(jnp.float32), dead, 64
    )
    order = order_matrix(lens_rank)
    region, sample = lens_region[0], lens_sample[0]
    labels = jnp.concatenate([region // 8, region % 8, sample], axis=0).astype(jnp.bfloat16)
    lens = jnp.concatenate([lens, labels], axis=0)
    columns = lax.dot_general(order, lens, nothing, preferred_element_type=jnp.float32)
    labels = columns[:, ZROWS + 2 :]
    region = (labels[:, 0] * 8.0 + labels[:, 1]).astype(jnp.int32)[None, :]
    sample = labels[:, 2:].astype(jnp.int32)
    place = columns[:, ZROWS : ZROWS + 2]
    wide = jnp.broadcast_to(place.T[:, :, None], (2, L_PATCH, LANES))
    place = place.reshape(LENS_TILES, SUB, 2)
    lens_box = jnp.stack([jnp.min(place, axis=1), jnp.max(place, axis=1)], axis=2)
    lens_box = jnp.pad(lens_box.reshape(LENS_TILES, 4).T, ((0, SUB - 4), (0, LANES - LENS_TILES)))
    where = jnp.stack([band, jnp.int32(bands)]).astype(jnp.int32)

    def pairs(blocks, shifts, before=None, last=False):
        return pair_sums(live, where, columns, wide, lens_box, blocks, shifts, before, last)

    sums = pairs([middle], (tuple((a, 0) for a in columns_at),))
    shifts = tuple(tuple((a, b) for a in columns_at) for b in (-1, 1))
    sums = pairs([below, above], shifts, sums, True)

    table = region_sums(region, sample, sums, regions_total)
    table = lax.all_to_all(table, axes, 0, 0, tiled=True)
    return owned_sums(table.reshape(-1, REG_DEV, WIDE))


def solution(mesh):
    placed = (
        P("ra", "dec", None, None),
        P("ra", "dec"),
        P("ra", "dec", None),
        P("ra", "dec", None),
        P("ra", "dec", None, None),
    )
    return jax.shard_map(
        on_device,
        mesh=mesh,
        in_specs=placed,
        out_specs=(P(("ra", "dec"), None, None), P(("ra", "dec"), None, None)),
        check_vma=False,
    )
```

```python
import functools
import math

import jax
import jax.numpy as jnp
import numpy as np
from jax import lax
from jax.experimental import pallas as pl
from jax.experimental.pallas import tpu as pltpu
from jax.sharding import PartitionSpec as P

NBIN = 20
SAMPLES = 8
PATCH = 256
R_IN = 12
L_PATCH = 512
S_PATCH = 1024
REG_DEV = 8
ZROWS = 128
LANES = 128
SUB = 8
SRC_TILES = S_PATCH // LANES
LENS_TILES = L_PATCH // SUB
UNROLL = (4, 4, 8)
CRIT_ROW = 5 * SUB
FAR = 1.0e6
BOX_ROW = ZROWS + SUB
BLOCK_ROWS = 144
LIST_WORDS = 16
LANE_SUMS = 22
FOLD_SPLIT = 32
VMEM_MIB = 26
THRESHOLD_SUMS = 2 * (NBIN + 1)
WIDE = 3 * LANES
growth_top = 23
growth_bottom = 20


def edge_squares():
    return [
        float((R_IN * growth_top**k // growth_bottom**k) ** 2) for k in range(NBIN + 1)
    ]


EDGES = edge_squares()
GROUPS = ((1, 10), (10, 16), (16, 21))


def lane_scales():
    lens_per_cell = L_PATCH / (SAMPLES * REG_DEV)
    density = S_PATCH / (PATCH * PATCH)
    expected = [
        math.pi * (EDGES[k + 1] - EDGES[k]) * density * lens_per_cell for k in range(NBIN)
    ]
    expected = np.array(expected, np.float32)
    row = np.ones((1, WIDE), np.float32)
    row[0, : 2 * NBIN * SAMPLES] = np.tile(np.stack([np.sqrt(expected), expected]).ravel(), SAMPLES)
    return jnp.asarray(row)


def tree_sum(terms):
    while len(terms) > 1:
        paired = [a + b for a, b in zip(terms[::2], terms[1::2])]
        terms = paired + ([terms[-1]] if len(terms) % 2 else [])
    return terms[0]


def spatial_order(x, y, dead, group):
    n = x.shape[0]
    index = jnp.arange(n, dtype=jnp.float32)
    key = x * n + index + dead * 2.0**20
    rank = jnp.sum((key[:, None] < key[None, :]).astype(jnp.float32), axis=0)
    key = jnp.floor(rank / group) * 2.0**18 + y * n + index
    return jnp.sum((key[:, None] < key[None, :]).astype(jnp.float32), axis=0)


def order_matrix(rank):
    n = rank.shape[0]
    target = lax.broadcasted_iota(jnp.float32, (n, n), 0)
    return (target == rank[None, :]).astype(jnp.bfloat16)


def column_of(row):
    return jnp.transpose(jnp.broadcast_to(row, (LANES, row.shape[1])))


def row_ranks(row):
    column = column_of(row)
    ranks = []
    for first in range(0, row.shape[1], LANES):
        below = jnp.where(column < row[:, first : first + LANES], 1.0, 0.0)
        ranks.append(jnp.sum(below, axis=0, keepdims=True))
    return jnp.concatenate(ranks, axis=1)


def source_kernel(source_ref, out_ref):
    n = S_PATCH
    index = lax.broadcasted_iota(jnp.int32, (1, n), 1).astype(jnp.float32)
    place = source_ref[ZROWS : ZROWS + 2, :].astype(jnp.float32)
    rank = row_ranks(place[0:1] * n + index)
    key = jnp.floor(rank * (1.0 / 256)) * 2.0**18 + place[1:2] * n + index
    rank = column_of(row_ranks(key))
    lane = lax.broadcasted_iota(jnp.int32, (n, LANES), 1).astype(jnp.float32)
    row = lax.broadcasted_iota(jnp.int32, (SRC_TILES, LANES), 0)
    boxes = [jnp.zeros((SRC_TILES, LANES), jnp.float32) for _ in range(4)]
    for first in range(0, n, 2 * LANES):
        match = jnp.concatenate(
            [jnp.where(rank == lane + float(first + at), 1.0, 0.0) for at in (0, LANES)], axis=1
        )
        ordered = jnp.dot(
            source_ref[...], match.astype(jnp.bfloat16), preferred_element_type=jnp.float32
        )
        out_ref[: ZROWS + 5, first : first + 2 * LANES] = ordered.astype(jnp.bfloat16)
        for at in (0, LANES):
            for c in range(4):
                values = ordered[ZROWS + c // 2 : ZROWS + c // 2 + 1, at : at + LANES]
                reduce = jnp.max if c % 2 else jnp.min
                bound = reduce(values, axis=1, keepdims=True)
                boxes[c] = jnp.where(row == (first + at) // LANES, bound, boxes[c])
    boxes = jnp.concatenate(boxes, axis=1).astype(jnp.bfloat16)
    out_ref[BOX_ROW:, : 4 * LANES] = boxes


def ordered_sources(source):
    vmem = pl.BlockSpec(memory_space=pltpu.VMEM)
    return pl.pallas_call(
        source_kernel,
        out_shape=jax.ShapeDtypeStruct((BLOCK_ROWS, S_PATCH), jnp.bfloat16),
        in_specs=[vmem],
        out_specs=vmem,
        compiler_params=pltpu.CompilerParams(vmem_limit_bytes=VMEM_MIB << 20),
        name="order_sources",
    )(source)


def tile_lists(lens_box, boxes, valid, tiles):
    wide = (tiles, LANES)
    gap_x = jnp.maximum(boxes[0] - lens_box[1:2], lens_box[0:1] - boxes[1])
    gap_y = jnp.maximum(boxes[2] - lens_box[3:4], lens_box[2:3] - boxes[3])
    gap_x, gap_y = jnp.maximum(gap_x, 0.0), jnp.maximum(gap_y, 0.0)
    near_sq = jnp.where(valid, gap_x * gap_x + gap_y * gap_y, FAR)
    lower = lax.broadcasted_iota(jnp.int32, (tiles, tiles), 0)
    lower = (lower >= lax.broadcasted_iota(jnp.int32, (tiles, tiles), 1)).astype(jnp.float32)
    lower = lower.astype(jnp.bfloat16)
    tile_id = lax.broadcasted_iota(jnp.int32, wide, 0).astype(jnp.float32) - tiles
    place = jnp.full(wide, -1.0, jnp.float32)
    base = jnp.zeros((1, LANES), jnp.float32)
    inner = jnp.zeros(wide, jnp.float32)
    trips = []
    for group, (_, hi) in enumerate(GROUPS):
        reach = (near_sq < EDGES[hi - 1]).astype(jnp.float32)
        member = (reach - inner).astype(jnp.bfloat16)
        running = jnp.dot(lower, member, preferred_element_type=jnp.float32)
        place = jnp.where(reach > inner, running + (base - 1.0), place)
        inner = reach
        base = base + running[tiles - 1 :]
        trips.append(jnp.floor((base + (UNROLL[group] - 1)) * (1.0 / UNROLL[group])))
    partial = []
    for slot in range(tiles):
        hit = jnp.where(place == float(slot), tile_id, 0.0)
        partial.append(tree_sum([hit[r : r + SUB] for r in range(0, tiles, SUB)]))
    partial = jnp.concatenate(partial, axis=0).astype(jnp.bfloat16)
    words = LIST_WORDS
    row = lax.broadcasted_iota(jnp.int32, (2 * words, tiles * SUB), 0)
    slot = lax.broadcasted_iota(jnp.int32, (2 * words, tiles * SUB), 1) >> 3
    first = 4 * (row & (words - 1)) + 2 * (row >> 4)
    take = jnp.where(slot == first, 1.0, jnp.where(slot == first + 1, 128.0, 0.0))
    packed = jnp.dot(take.astype(jnp.bfloat16), partial, preferred_element_type=jnp.float32)
    packed = (packed + 129.0 * tiles).astype(jnp.int32)
    packed = packed[:words] + packed[words:] * (1 << 14)
    row = lax.broadcasted_iota(jnp.int32, (SUB, LANES), 0)
    counts = jnp.where(row == 0, trips[0], jnp.where(row == 1, trips[1], trips[2]))
    return jnp.concatenate([packed, counts.astype(jnp.int32)], axis=0)


def pair_kernel(shifts, later, last, *refs):
    n = sum(len(group) for group in shifts)
    tiles = n * SRC_TILES
    live_ref, band_ref, columns_ref, place_ref, box_ref = refs[:5]
    blocks = refs[5 : 5 + len(shifts)]
    rest = refs[5 + len(shifts) :]
    before_ref = None
    if later:
        before_ref, *rest = rest
    if last:
        fold_ref, out_ref, *rest = rest
    sums, *rest = rest
    tables, slots, list_vmem, list_ref, list_sem = rest
    live = live_ref[0]
    tile_shape = (SUB, LANES)
    patches = [
        (block, at, shift)
        for block, group in zip(blocks, shifts)
        for at, shift in enumerate(group)
    ]

    boxes, valid = [[] for _ in range(4)], []
    for block, at, shift in patches:
        for c in range(4):
            part = block[at, BOX_ROW : BOX_ROW + SUB, c * LANES : (c + 1) * LANES]
            boxes[c].append(part.astype(jnp.float32) + shift[c // 2] * PATCH)
        there = band_ref[0] + shift[1]
        inside = (there >= 0) & (there < band_ref[1])
        valid.append(jnp.full(tile_shape, inside.astype(jnp.float32)))
    boxes = [jnp.concatenate(box, axis=0) for box in boxes]
    valid = jnp.concatenate(valid, axis=0) > 0.0
    list_vmem[...] = tile_lists(box_ref[...], boxes, valid, tiles)
    copy = pltpu.make_async_copy(list_vmem, list_ref, list_sem)
    copy.start()

    for p, (block, at, (shift_x, shift_y)) in enumerate(patches):
        rows = block[at, ZROWS : ZROWS + 5, :].astype(jnp.float32)
        weight = rows[4:5]
        values = (
            rows[0:1] + shift_x * PATCH,
            rows[1:2] + shift_y * PATCH,
            -(weight * rows[2:3]),
            -2.0 * (weight * rows[3:4]),
            weight,
        )
        for t in range(SRC_TILES):
            for v, value in enumerate(values):
                tables[p * SRC_TILES + t, v * SUB : (v + 1) * SUB] = jnp.broadcast_to(
                    value[:, t * LANES : (t + 1) * LANES], tile_shape
                )
    for v in range(5):
        tables[tiles, v * SUB : (v + 1) * SUB] = jnp.full(
            tile_shape, FAR if v == 0 else 0.0, jnp.float32
        )
    tables[tiles, CRIT_ROW:] = jnp.zeros((L_PATCH, LANES), jnp.float32)

    def crit_step(chunk, carry):
        first = pl.multiple_of(chunk * LANES, LANES)
        kernel_rows = columns_ref[pl.ds(first, LANES), :ZROWS].astype(jnp.bfloat16)
        for p, (block, at, _) in enumerate(patches):
            product = jnp.dot(
                kernel_rows, block[at, :ZROWS, :], preferred_element_type=jnp.float32
            )
            for t in range(SRC_TILES):
                tables[p * SRC_TILES + t, pl.ds(CRIT_ROW + first, LANES), :] = product[
                    :, t * LANES : (t + 1) * LANES
                ]
        return carry

    lax.fori_loop(0, (live + LANES - 1) // LANES, crit_step, 0)
    copy.wait()

    def add_up(rows, terms, group):
        for k in range(*GROUPS[group]):
            inside = [r2 < EDGES[k] for _, _, r2 in terms]
            for c in range(2):
                picked = [jnp.where(m, t[c], 0.0) for m, t in zip(inside, terms)]
                at = c * (NBIN + 1) + k
                sums[at, rows, :] = sums[at, rows, :] + tree_sum(picked)

    def lens_step(lens_tile, base):
        first = pl.multiple_of(lens_tile * SUB, SUB)
        rows = pl.ds(pl.multiple_of(first - base, SUB), SUB)
        trips = [list_ref[LIST_WORDS + group, lens_tile] for group in range(3)]
        lens_x = place_ref[0, pl.ds(first, SUB), :]
        lens_y = place_ref[1, pl.ds(first, SUB), :]
        for v in range(THRESHOLD_SUMS):
            sums[v, rows, :] = (
                before_ref[v, pl.ds(first, SUB), :] if later else jnp.zeros(tile_shape, jnp.float32)
            )

        def far_step(i, words):
            following = (list_ref[2 * i + 2, lens_tile], list_ref[2 * i + 3, lens_tile])
            terms = []
            for u in range(UNROLL[2]):
                tile = (words[u // 4] >> (7 * (u % 4))) & 127
                dx, dy = tables[tile, 0:SUB] - lens_x, tables[tile, SUB : 2 * SUB] - lens_y
                dx_sq, dy_sq = dx * dx, dy * dy
                r2 = dx_sq + dy_sq
                r2 = jnp.where(r2 >= EDGES[0], r2, FAR)
                turned = tables[tile, 2 * SUB : 3 * SUB] * (dx_sq - dy_sq)
                turned = turned + tables[tile, 3 * SUB : 4 * SUB] * (dx * dy)
                value = tables[tile, pl.ds(CRIT_ROW + first, SUB), :]
                signal = value * (turned / r2)
                weight = tables[tile, 4 * SUB : 5 * SUB] * value * value
                slots[0, i * UNROLL[2] + u] = signal
                slots[1, i * UNROLL[2] + u] = weight
                slots[2, i * UNROLL[2] + u] = r2
                terms.append((signal, weight, r2))
            add_up(rows, terms, 2)
            return following

        lax.fori_loop(0, trips[2], far_step, (list_ref[0, lens_tile], list_ref[1, lens_tile]))
        for group in (1, 0):

            def near_step(i, nothing, group=group):
                terms = [
                    tuple(slots[c, i * UNROLL[group] + u] for c in range(3))
                    for u in range(UNROLL[group])
                ]
                add_up(rows, terms, group)
                return nothing

            lax.fori_loop(0, trips[group], near_step, 0)
        return base

    lens_tiles = live // SUB
    if not last:
        lax.fori_loop(0, lens_tiles, lens_step, 0)
        return
    out_ref[...] = jnp.zeros_like(out_ref)

    def chunk_step(chunk, carry):
        first = pl.multiple_of(chunk * LANES, LANES)
        tiles_first = chunk * (LANES // SUB)
        tiles_end = jnp.minimum(tiles_first + LANES // SUB, lens_tiles)
        lax.fori_loop(tiles_first, tiles_end, lens_step, first)
        high, low = [], []
        for v in range(LANE_SUMS, THRESHOLD_SUMS):
            value = sums[v]
            high.append(value.astype(jnp.bfloat16))
            low.append((value - high[-1].astype(jnp.float32)).astype(jnp.bfloat16))
        folded = []
        for lo, hi in ((LANE_SUMS, FOLD_SPLIT), (FOLD_SPLIT, THRESHOLD_SUMS)):
            both = [
                jnp.concatenate(part[lo - LANE_SUMS : hi - LANE_SUMS], axis=1)
                for part in (high, low)
            ]
            weights = fold_ref[lo * LANES : hi * LANES, :]
            folded += [jnp.dot(p, weights, preferred_element_type=jnp.float32) for p in both]
        folded = tree_sum(folded)
        lane = lax.broadcasted_iota(jnp.int32, (LANES, LANES), 1)
        for v in range(LANE_SUMS):
            folded = jnp.where(lane == v, jnp.sum(sums[v], axis=1, keepdims=True), folded)
        row = lax.broadcasted_iota(jnp.int32, (LANES, LANES), 0) + first
        folded = jnp.where(row < live, folded, 0.0)
        out_ref[pl.ds(first, LANES), :] = folded
        return carry

    lax.fori_loop(0, (live + LANES - 1) // LANES, chunk_step, 0)


def fold_matrix():
    matrix = np.zeros((THRESHOLD_SUMS, LANES, LANES), np.float32)
    for v in range(THRESHOLD_SUMS):
        matrix[v, :, v] = 1.0
    return jnp.asarray(matrix.reshape(-1, LANES), jnp.bfloat16)


def pair_sums(live, bands, columns, place, lens_box, blocks, shifts, before=None, last=False):
    n = sum(len(group) for group in shifts)
    tiles = n * SRC_TILES
    later = before is not None
    smem = pl.BlockSpec(memory_space=pltpu.SMEM)
    vmem = pl.BlockSpec(memory_space=pltpu.VMEM)
    all_sums = (THRESHOLD_SUMS, L_PATCH, LANES)
    scratch = [
        pltpu.VMEM((tiles + 1, CRIT_ROW + L_PATCH, LANES), jnp.float32),
        pltpu.VMEM((3, tiles, SUB, LANES), jnp.float32),
        pltpu.VMEM((LIST_WORDS + SUB, LANES), jnp.int32),
        pltpu.SMEM((LIST_WORDS + SUB, LANES), jnp.int32),
        pltpu.SemaphoreType.DMA,
    ]
    operands = (live, bands, columns, place, lens_box, *blocks)
    operands += (before,) if later else ()
    operands += (fold_matrix(),) if last else ()
    return pl.pallas_call(
        functools.partial(pair_kernel, shifts, later, last),
        out_shape=jax.ShapeDtypeStruct((L_PATCH, LANES) if last else all_sums, jnp.float32),
        in_specs=[smem] * 2 + [vmem] * (len(operands) - 2),
        out_specs=vmem,
        input_output_aliases={5 + len(blocks): 0} if later and not last else {},
        scratch_shapes=([pltpu.VMEM((THRESHOLD_SUMS, LANES, LANES), jnp.float32)] if last else []) + scratch,
        cost_estimate=pl.CostEstimate(
            flops=n * 20_000_000_000, transcendentals=0, bytes_accessed=n * 300_000
        ),
        compiler_params=pltpu.CompilerParams(vmem_limit_bytes=VMEM_MIB << 20),
        name=f"pairs_{n}",
    )(*operands)


def split_parts(value):
    parts = []
    for _ in range(3):
        part = value.astype(jnp.bfloat16)
        value = value - part.astype(jnp.float32)
        parts.append(part)
    return parts


def bin_placement():
    matrix = np.zeros((LANES, WIDE), np.float32)
    for m in range(SAMPLES):
        for c in range(2):
            for k in range(NBIN):
                column = (m * 2 + c) * NBIN + k
                matrix[c * (NBIN + 1) + k + 1, column] = 1.0
                matrix[c * (NBIN + 1) + k, column] = -1.0
    return jnp.asarray(matrix, jnp.bfloat16)


def table_kernel(region_ref, sample_ref, sums_ref, place_ref, out_ref):
    def product(matrices, others):
        return tree_sum(
            [jnp.dot(a, b, preferred_element_type=jnp.float32) for a, b in zip(matrices, others)][::-1]
        )

    bins = product(split_parts(sums_ref[...]), [place_ref[...]] * 3)
    lane = lax.broadcasted_iota(jnp.int32, bins.shape, 1) - sample_ref[...] * (2 * NBIN)
    bins = jnp.where((lane >= 0) & (lane < 2 * NBIN), bins, 0.0)
    region = region_ref[...]
    ids = lax.broadcasted_iota(jnp.int32, (out_ref.shape[0], region.shape[1]), 0)
    match = (ids == region).astype(jnp.float32).astype(jnp.bfloat16)
    out_ref[...] = product([match] * 2, split_parts(bins)[:2])


def region_sums(region, sample, sums, regions_total):
    vmem = pl.BlockSpec(memory_space=pltpu.VMEM)
    return pl.pallas_call(
        table_kernel,
        out_shape=jax.ShapeDtypeStruct((regions_total, WIDE), jnp.float32),
        in_specs=[vmem] * 4,
        out_specs=vmem,
        compiler_params=pltpu.CompilerParams(vmem_limit_bytes=VMEM_MIB << 20),
        name="region_table",
    )(region, sample, sums, bin_placement())


def owned_kernel(parts_ref, scale_ref, signal_ref, weight_ref):
    total = jnp.sum(parts_ref[...], axis=0) / scale_ref[...]
    for m in range(SAMPLES):
        for c, out_ref in enumerate((signal_ref, weight_ref)):
            first = (2 * m + c) * NBIN
            out_ref[:, m, :] = total[:, first : first + NBIN]


def owned_sums(parts):
    vmem = pl.BlockSpec(memory_space=pltpu.VMEM)
    out = jax.ShapeDtypeStruct((REG_DEV, SAMPLES, NBIN), jnp.float32)
    return pl.pallas_call(
        owned_kernel,
        out_shape=(out, out),
        in_specs=[vmem] * 2,
        out_specs=(vmem, vmem),
        compiler_params=pltpu.CompilerParams(vmem_limit_bytes=VMEM_MIB << 20),
        name="owned_sums",
    )(parts, lane_scales())


def shifted(block, axis, periodic):
    count = lax.axis_size(axis)
    forward = [(i, i + 1) for i in range(count - 1)]
    if periodic:
        forward.append((count - 1, 0))
    backward = [(b, a) for a, b in forward]
    return lax.ppermute(block, axis, forward), lax.ppermute(block, axis, backward)


def on_device(lens_block, lens_count, lens_region, lens_sample, source_block):
    axes = ("ra", "dec")
    bands, band = lax.axis_size("dec"), lax.axis_index("dec")
    regions_total = REG_DEV * lax.axis_size("ra") * bands
    nothing = (((1,), (1,)), ((), ()))

    source = ordered_sources(source_block[0, 0])
    low, high = shifted(source, "ra", True)
    middle = jnp.stack([source, low, high])
    columns_at = (0, -1, 1)
    with jax.named_scope("halo_dec"):
        below, above = shifted(middle, "dec", False)

    lens = lens_block[0, 0]
    live = lens_count[0]
    dead = (jnp.arange(L_PATCH, dtype=jnp.int32) >= live[0]).astype(jnp.float32)
    lens_rank = spatial_order(
        lens[ZROWS].astype(jnp.float32), lens[ZROWS + 1].astype(jnp.float32), dead, 64
    )
    order = order_matrix(lens_rank)
    region, sample = lens_region[0], lens_sample[0]
    labels = jnp.concatenate([region // 8, region % 8, sample], axis=0).astype(jnp.bfloat16)
    lens = jnp.concatenate([lens, labels], axis=0)
    columns = lax.dot_general(order, lens, nothing, preferred_element_type=jnp.float32)
    labels = columns[:, ZROWS + 2 :]
    region = (labels[:, 0] * 8.0 + labels[:, 1]).astype(jnp.int32)[None, :]
    sample = labels[:, 2:].astype(jnp.int32)
    place = columns[:, ZROWS : ZROWS + 2]
    wide = jnp.broadcast_to(place.T[:, :, None], (2, L_PATCH, LANES))
    place = place.reshape(LENS_TILES, SUB, 2)
    lens_box = jnp.stack([jnp.min(place, axis=1), jnp.max(place, axis=1)], axis=2)
    lens_box = jnp.pad(lens_box.reshape(LENS_TILES, 4).T, ((0, SUB - 4), (0, LANES - LENS_TILES)))
    where = jnp.stack([band, jnp.int32(bands)]).astype(jnp.int32)

    def pairs(blocks, shifts, before=None, last=False):
        return pair_sums(live, where, columns, wide, lens_box, blocks, shifts, before, last)

    sums = pairs([middle], (tuple((a, 0) for a in columns_at),))
    shifts = tuple(tuple((a, b) for a in columns_at) for b in (-1, 1))
    sums = pairs([below, above], shifts, sums, True)

    table = region_sums(region, sample, sums, regions_total)
    table = lax.all_to_all(table, axes, 0, 0, tiled=True)
    return owned_sums(table.reshape(-1, REG_DEV, WIDE))


def solution(mesh):
    placed = (
        P("ra", "dec", None, None),
        P("ra", "dec"),
        P("ra", "dec", None),
        P("ra", "dec", None),
        P("ra", "dec", None, None),
    )
    return jax.shard_map(
        on_device,
        mesh=mesh,
        in_specs=placed,
        out_specs=(P(("ra", "dec"), None, None), P(("ra", "dec"), None, None)),
        check_vma=False,
    )
```
